128 devices in a mesh: slab: 64 (over z, y, x), col: 2 (over core).
Axes of the slice: x: 4, y: 4, z: 4, core: 2. Of those that a mesh axis runs over, the one named last changes fastest.
Arguments:
- coupling: float32 [64, 512, 512], P('slab', None, 'col'), as said below
- tile_pattern: int32 [64, 4, 4], P('slab', None, 'col'), may hold values from 0 to 1, as said below
- orbital_mass: float32 [64, 512], P('slab', 'col'), may hold values from 0.0001 to 0.05
- sources: float32 [64, 512, 256], P('slab', None, 'col'), may hold values from -0.3 to 0.3
Outputs:
- solution: float32 [64, 512, 256], P('slab', None, 'col')
The draws below stay inside these ranges and needn't reach their ends.
Inputs may be any that keep to these rules, and one draw needn't show every extreme that they name: Each coupling block is symmetric and positive semidefinite. `tile_pattern`: in each slab every tile belongs to one group, and two tiles are linked exactly when they share a group, so each pattern is symmetric with ones on its diagonal.
All inputs are finite; a program needn't handle non-finite values.
Results may differ from the reference program's by a relative error of at most 0.0003.
Values sent between devices are 32-bit elements; how exact they have to be, the bound alone decides.
A program may use at most 128 MiB of HBM per device.

```python
import math
import jax
import jax.numpy as jnp
from jax import lax

ORBITALS = 512
TILE = 128
TILES = 4
MODES = 256
LEVELS = 6
SLABS = 64


def draw_coupling(key, part):
    raw = jnp.clip(jax.random.normal(key, (SLABS, ORBITALS, ORBITALS), jnp.float32), -3.0, 3.0)
    product = jnp.matmul(raw, jnp.swapaxes(raw, 1, 2), precision=lax.Precision.HIGHEST)
    return (product + jnp.swapaxes(product, 1, 2)) * (1.5 / ORBITALS)


def draw_tile_pattern(key, part):
    groups = jax.random.randint(key, (SLABS, TILES), 0, TILES).astype(jnp.int32)
    return (groups[:, :, None] == groups[:, None, :]).astype(jnp.int32)


def shard_levels(key, shape, shards, least, largest):
    level = 1.0
    for dim, blocks in shards:
        draws = jax.random.uniform(jax.random.fold_in(jax.random.fold_in(key, 6), dim), (blocks,), jnp.float32, least / len(shards), largest / len(shards))
        level = level * jnp.repeat(jnp.exp(draws), shape[dim] // blocks).reshape((-1,) + (1,) * (len(shape) - 1 - dim))
    return level


def normal_values(own_key, dims, spread, reach, pieces=(), kind=jnp.bfloat16):
    drawn = spread * jax.random.normal(own_key, dims, jnp.float32)
    if pieces:
        drawn = drawn * shard_levels(own_key, dims, pieces, -0.22, 0.18)
    return jnp.clip(drawn, -reach, reach).astype(kind)


def setup_inputs(seed: int = 0) -> dict:
    key_of = jax.random.split(jax.random.key(seed), 5)
    return {
        "coupling": draw_coupling(jax.random.fold_in(key_of[4], 71), 0),
        "tile_pattern": draw_tile_pattern(jax.random.fold_in(key_of[4], 71), 0),
        "orbital_mass": jnp.clip(jnp.exp(math.log(0.05) - 6.214608 * jax.random.uniform(key_of[2], (SLABS, ORBITALS), jnp.float32) ** shard_levels(key_of[2], (SLABS, ORBITALS), ((0, 64), (1, 2)), -0.2, 0.2)), 0.0001, 0.05),
        "sources": normal_values(key_of[3], (SLABS, ORBITALS, MODES), 0.05, 0.3, ((0, 64), (2, 2)), jnp.float32),
    }


leaf_limit = 128

def factor_inverse(matrix):
    width = matrix.shape[-1]
    if width <= leaf_limit:
        factor = jnp.linalg.cholesky(matrix)
        unit = jnp.broadcast_to(jnp.eye(width, dtype=matrix.dtype), matrix.shape)
        return lax.linalg.triangular_solve(factor, unit, left_side=True, lower=True)
    half_w = width // 2
    top_left = matrix[..., :half_w, :half_w]
    bottom_left = matrix[..., half_w:, :half_w]
    bottom_right = matrix[..., half_w:, half_w:]
    first_inv = factor_inverse(top_left)
    lower_part = jnp.matmul(bottom_left, jnp.swapaxes(first_inv, -1, -2), precision=lax.Precision.HIGHEST)
    schur_part = bottom_right - jnp.matmul(lower_part, jnp.swapaxes(lower_part, -1, -2), precision=lax.Precision.HIGHEST)
    second_inv = factor_inverse(schur_part)
    cross = -jnp.matmul(second_inv, jnp.matmul(lower_part, first_inv, precision=lax.Precision.HIGHEST), precision=lax.Precision.HIGHEST)
    upper_row = jnp.concatenate([first_inv, jnp.zeros_like(lower_part.swapaxes(-1, -2))], axis=-1)
    lower_row = jnp.concatenate([cross, second_inv], axis=-1)
    return jnp.concatenate([upper_row, lower_row], axis=-2)

def solve_spd(matrix, rhs):
    inverse = factor_inverse(matrix)
    inner = jnp.matmul(inverse, rhs, precision=lax.Precision.HIGHEST)
    return jnp.matmul(jnp.swapaxes(inverse, -1, -2), inner, precision=lax.Precision.HIGHEST)

def reference(coupling, tile_pattern, orbital_mass, sources):
    count = coupling.shape[0]
    width = coupling.shape[1]
    tile_mask = jnp.repeat(jnp.repeat(tile_pattern, TILE, axis=1), TILE, axis=2).astype(jnp.float32)
    unit = jnp.eye(width, dtype=jnp.float32)
    bond = unit[None] + tile_mask * coupling
    prior = jnp.concatenate([jnp.zeros_like(bond[:1]), bond[:-1]], axis=0)
    keep_upper = (jnp.arange(count) < count - 1).astype(jnp.float32)[:, None, None]
    lower_blk = -prior
    upper_blk = -bond * keep_upper
    diag_blk = bond + prior + unit[None] * orbital_mass[:, None, :]
    source = sources
    for level_num in range(LEVELS):
        stride = 2 ** level_num
        if stride >= count:
            break
        solved = solve_spd(diag_blk, jnp.concatenate([upper_blk, lower_blk, source], axis=2))
        padding = jnp.zeros_like(solved[:stride])
        from_below = jnp.concatenate([padding, solved[:count - stride]], axis=0)
        from_above = jnp.concatenate([solved[stride:], padding], axis=0)
        below_prod = jnp.einsum('nij,njk->nik', lower_blk, from_below, precision=lax.Precision.HIGHEST)
        above_prod = jnp.einsum('nij,njk->nik', upper_blk, from_above, precision=lax.Precision.HIGHEST)
        diag_blk = diag_blk - below_prod[:, :, :width] - above_prod[:, :, width:2 * width]
        new_lower = -below_prod[:, :, width:2 * width]
        new_upper = -above_prod[:, :, :width]
        source = source - below_prod[:, :, 2 * width:] - above_prod[:, :, 2 * width:]
        lower_blk = new_lower
        upper_blk = new_upper
    return solve_spd(diag_blk, source)
```

```python
import functools

import jax
import jax.numpy as jnp
from jax import lax
from jax.experimental import pallas as pl
from jax.experimental.pallas import tpu as pltpu
from jax.sharding import PartitionSpec as P

F32 = jnp.float32
N = 512
H = 256
T = 128
M = 256
NT = (((1,), (1,)), ((), ()))
NN = (((1,), (0,)), ((), ()))
TILES = ((0, 0), (1, 0), (1, 1), (2, 0), (3, 0), (2, 1), (3, 1), (2, 2), (3, 2), (3, 3))
PIECES = ((0, 3), (3, 4), (7, 3))
MESH = pl.DeviceIdType.MESH


def dot(a, b, dims=NT):
    return lax.dot_general(
        a, b, dims, precision=lax.Precision.HIGHEST, preferred_element_type=F32
    )


def leaf(block, scr):
    rows = [block[8 * i : 8 * i + 8, :] for i in range(16)]
    lane = lax.broadcasted_iota(jnp.int32, (8, T), 1)
    sub = lax.broadcasted_iota(jnp.int32, (8, T), 0)
    out = []
    for J in range(16):
        b = (J % 2) * 9
        own = (lane >= 8 * J) & (lane < 8 * J + 8)
        for j in range(8):
            scr[b + j] = jnp.broadcast_to(rows[J][:, 8 * J + j : 8 * J + j + 1], (8, T))
        scr[b + 8] = jnp.where(own, jnp.where(lane == sub + 8 * J, 1.0, 0.0), rows[J])
        R = [jnp.broadcast_to(scr[b + 8, i : i + 1, :], (8, T)) for i in range(8)]
        E = [[None] * 8 for _ in range(8)]
        for i in range(8):
            for j in range(i + 1):
                E[i][j] = E[j][i] = jnp.broadcast_to(scr[b + j, i : i + 1, :], (8, T))
        V = [None] * 8
        for j in range(0, 8, 2):
            a, c, e = E[j][j], E[j][j + 1], E[j + 1][j + 1]
            q = 1.0 / (a * e - c * c)
            r = c * (1.0 / a)
            V[j] = R[j] * lax.rsqrt(a)
            V[j + 1] = (R[j + 1] - r * R[j]) * lax.rsqrt(e - c * r)
            ia, ic, ie = e * q, c * q, a * q
            R[j], R[j + 1] = ia * R[j] - ic * R[j + 1], ie * R[j + 1] - ic * R[j]
            for k in range(j + 2, 8):
                E[j][k], E[j + 1][k] = (
                    ia * E[j][k] - ic * E[j + 1][k],
                    ie * E[j + 1][k] - ic * E[j][k],
                )
            for i in range(8):
                if i in (j, j + 1):
                    continue
                m0, m1 = E[i][j], E[i][j + 1]
                R[i] = R[i] - (m0 * R[j] + m1 * R[j + 1])
                for k in range(j + 2, 8):
                    if i < j or k >= i:
                        E[i][k] = E[i][k] - (m0 * E[j][k] + m1 * E[j + 1][k])
            for i in range(j + 2, 8):
                for k in range(j + 2, i):
                    E[i][k] = E[k][i]
        for i in range(J + 1, 16):
            t = None
            for k in range(8):
                c = jnp.broadcast_to(rows[i][:, 8 * J + k : 8 * J + k + 1], (8, T)) * R[k]
                t = c if t is None else t + c
            rows[i] = jnp.where(own, 0.0, rows[i]) - t
        z = V[0]
        for r in range(1, 8):
            z = jnp.where(sub == r, V[r], z)
        out.append(jnp.where(lane <= sub + 8 * J, z, 0.0))
    return jnp.concatenate(out, 0)


def kernel(
    slabs,
    levels,
    brow,
    srct,
    mrow,
    out,
    recvP,
    recvQ,
    sibQ,
    recvR,
    sibR,
    VY,
    O,
    VX,
    VR,
    RT,
    D,
    DW,
    T2,
    G,
    W,
    scr,
    mb,
    sendQ,
    sendP,
    sendR,
    i_send,
    i_recv,
    n_send,
    n_recv,
    f_send,
    f_recv,
    v_send,
    v_recv,
    q_send,
    q_recv,
    qf_send,
    qf_recv,
    p_send,
    p_recv,
    r_send,
    r_recv,
    rf_send,
    rf_recv,
):
    s = lax.axis_index("slab")
    c = lax.axis_index("col")
    sgn = 2 * c - 1
    sib = 1 - c

    def inside(t):
        return (t >= 0) & (t < slabs)

    def remote(src, dst, ss, rs, slab, col):
        return pltpu.make_async_remote_copy(
            src_ref=src,
            dst_ref=dst,
            send_sem=ss,
            recv_sem=rs,
            device_id={"slab": slab, "col": col},
            device_id_type=MESH,
        )

    barrier = pltpu.get_barrier_semaphore()
    pl.semaphore_signal(barrier, inc=1, device_id={"slab": s, "col": sib}, device_id_type=MESH)
    count = 1
    for k in range(levels):
        peer = s + sgn * 2**k
        here = inside(peer)
        count = count + here.astype(jnp.int32)

        @pl.when(here)
        def _():
            pl.semaphore_signal(
                barrier, inc=1, device_id={"slab": peer, "col": sib}, device_id_type=MESH
            )

    pl.semaphore_wait(barrier, count)

    first = recvP.at[0]
    own_rt = pl.ds(pl.multiple_of(c * T, T), T)
    RT[own_rt, :] = srct[...]
    to_sib = functools.partial(remote, slab=s, col=sib)
    cp_m = to_sib(mrow, mb, i_send.at[0], i_recv.at[0])
    cp_r = to_sib(srct, RT.at[own_rt], i_send.at[1], i_recv.at[1])
    low, high = pl.ds(0, H), pl.ds(H, H)
    cp_b0 = to_sib(brow, first.at[low], i_send.at[2], i_recv.at[2])
    cp_b1 = to_sib(brow, O.at[high], i_send.at[2], i_recv.at[2])
    nxt = [
        remote(first.at[h], first.at[h], n_send.at[i], n_recv.at[i], s + 1, 0)
        for i, h in enumerate((low, high))
    ]
    fwd = [
        to_sib(first.at[h], O.at[h], f_send.at[i], f_recv.at[i]) for i, h in enumerate((low, high))
    ]

    @pl.when(c == 0)
    def _():
        cp_b0.start()
        O[0:H, :] = brow[...]

    @pl.when(c == 1)
    def _():
        cp_b1.start()
        first[H:N, :] = brow[...]

    cp_m.start()
    cp_r.start()

    @pl.when(c == 1)
    def _():
        cp_b0.wait_recv()

        @pl.when(s < slabs - 1)
        def _():
            nxt[0].start()
            nxt[1].start()

        @pl.when(s > 0)
        def _():
            fwd[0].wait_recv()
            fwd[1].wait_recv()

        @pl.when(s == 0)
        def _():
            O[...] = jnp.zeros((N, N), F32)

        cp_b1.wait_send()

    @pl.when(c == 0)
    def _():
        @pl.when(s > 0)
        def _():
            nxt[0].wait_recv()
            fwd[0].start()
            nxt[1].wait_recv()
            fwd[1].start()

        @pl.when(s == 0)
        def _():
            first[...] = jnp.zeros((N, N), F32)

        cp_b1.wait_recv()
        cp_b0.wait_send()

    cp_m.wait()
    mass = mrow[0:1, :] + mb[0:1, :]
    eye = lax.broadcasted_iota(jnp.int32, (T, T), 0) == lax.broadcasted_iota(jnp.int32, (T, T), 1)
    for n, (i, j) in enumerate(TILES):
        rr, cc = slice(T * i, T * i + T), slice(T * j, T * j + T)
        tile = first[rr, cc] + O[rr, cc]
        if i == j:
            tile = tile + jnp.where(eye, jnp.broadcast_to(mass[:, cc], (T, T)), 0.0)
        D[n] = tile
    cp_r.wait()

    @pl.when((c == 1) & (s < slabs - 1))
    def _():
        nxt[0].wait_send()
        nxt[1].wait_send()

    @pl.when((c == 0) & (s > 0))
    def _():
        fwd[0].wait_send()
        fwd[1].wait_send()

    @pl.when(jnp.logical_not(inside(s + sgn)))
    def _():
        first[...] = jnp.zeros((N, N), F32)

    T2[...] = jnp.zeros((2, H, H), F32)

    def step(k, d):
        prev = d // 2
        e = inside(s + sgn * d) & (k < levels)
        e_prev = inside(s + sgn * prev) & (k >= 1)
        e_sib = inside(s - sgn * prev) & (k >= 1)
        kp = jnp.maximum(k - 1, 0)
        peer = s + sgn * d
        peer_prev = s + sgn * prev

        def q_copy(p, level, to):
            o, n = PIECES[p]
            return remote(
                sendQ.at[pl.ds(o, n)],
                recvQ.at[level, pl.ds(o, n)],
                q_send.at[p],
                q_recv.at[level, p],
                to,
                sib,
            )

        def q_forward(p, level):
            o, n = PIECES[p]
            return to_sib(
                recvQ.at[level, pl.ds(o, n)],
                sibQ.at[level, pl.ds(o, n)],
                qf_send.at[p],
                qf_recv.at[level, p],
            )

        def p_copy(h, level, to):
            rows = pl.ds(pl.multiple_of(h * H, H), H)
            return remote(
                sendP.at[rows],
                recvP.at[level + 1, rows],
                p_send.at[h],
                p_recv.at[level, h],
                to,
                sib,
            )

        def v_copy(h, level):
            rows = pl.ds(pl.multiple_of(h * H, H), H)
            return to_sib(VX.at[rows], VY.at[level, rows], v_send.at[h], v_recv.at[level, h])

        def r_copy(level, to):
            return remote(sendR, recvR.at[level], r_send, r_recv.at[level], to, sib)

        def r_forward(level):
            return to_sib(recvR.at[level], sibR.at[level], rf_send, rf_recv.at[level])

        def take(p):
            o, n = PIECES[p]

            @pl.when(e_prev)
            def _():
                q_copy(p, kp, peer_prev).wait_recv()
                q_forward(p, kp).start()
                D[o : o + n] = D[o : o + n] - recvQ[kp, o : o + n]

            @pl.when(e_sib)
            def _():
                q_forward(p, kp).wait_recv()
                D[o : o + n] = D[o : o + n] - sibQ[kp, o : o + n]

            DW[o : o + n] = D[o : o + n]

            @pl.when(e_prev)
            def _():
                q_forward(p, kp).wait_send()

        take(0)

        def quarter(i, _):
            h = i // 2
            inv = leaf(DW[7 * h + 2 * (i - 2 * h)], scr)

            @pl.when(i == 2 * h)
            def _():
                T2[h, 0:T, 0:T] = inv
                g = dot(DW[7 * h + 1], inv)
                DW[7 * h + 2] = DW[7 * h + 2] - dot(g, g)
                W[...] = dot(g, inv, NN)

            @pl.when(i == 2 * h + 1)
            def _():
                T2[h, T:H, T:H] = inv
                T2[h, T:H, 0:T] = -dot(inv, W[...], NN)

            @pl.when(i == 1)
            def _():
                take(1)
                ba = jnp.concatenate(
                    [
                        jnp.concatenate([DW[3], DW[5]], 1),
                        jnp.concatenate([DW[4], DW[6]], 1),
                    ],
                    0,
                )
                g = dot(ba, T2[0])
                G[...] = g
                gg = dot(g, g)
                take(2)
                DW[7] = DW[7] - gg[0:T, 0:T]
                DW[8] = DW[8] - gg[T:H, 0:T]
                DW[9] = DW[9] - gg[T:H, T:H]

            return 0

        lax.fori_loop(0, 4, quarter, 0)

        @pl.when(k < levels)
        def _():
            def solve(h, _):
                rows = pl.ds(pl.multiple_of(h * H, H), H)

                @pl.when(e_prev)
                def _():
                    p_copy(h, kp, peer_prev).wait_recv()

                @pl.when((k >= 1))
                def _():
                    v_copy(h, kp).wait_send()

                va = dot(recvP[k, rows, 0:H], T2[0])
                VX[rows, 0:H] = va
                VX[rows, H:N] = dot(recvP[k, rows, H:N] - dot(va, G[...]), T2[1])

                @pl.when(k < levels - 1)
                def _():
                    v_copy(h, k).start()

                return 0

            lax.fori_loop(0, 2, solve, 0)

            for p, (i, j) in enumerate(((0, 0), (1, 0), (1, 1))):
                qq = dot(VX[i * H : i * H + H, :], VX[j * H : j * H + H, :])

                @pl.when(e_prev)
                def _():
                    q_copy(p, kp, peer_prev).wait_send()

                for n in range(PIECES[p][0], PIECES[p][0] + PIECES[p][1]):
                    r0, c0 = TILES[n][0] * T - i * H, TILES[n][1] * T - j * H
                    sendQ[n] = qq[r0 : r0 + T, c0 : c0 + T]

                @pl.when(e)
                def _():
                    q_copy(p, k, peer).start()

        @pl.when(k < levels - 1)
        def _():
            def product(h, _):
                rows = pl.ds(pl.multiple_of(h * H, H), H)
                v_copy(h, k).wait_recv()

                @pl.when(e_prev)
                def _():
                    p_copy(h, kp, peer_prev).wait_send()

                sendP[rows, :] = dot(VY[k, rows, :], VX[...])

                @pl.when(e)
                def _():
                    p_copy(h, k, peer).start()

                @pl.when(jnp.logical_not(e))
                def _():
                    recvP[k + 1, rows, :] = jnp.zeros((H, N), F32)

                return 0

            lax.fori_loop(0, 2, product, 0)

        @pl.when((k == levels - 1) & e_prev)
        def _():
            p_copy(0, kp, peer_prev).wait_send()
            p_copy(1, kp, peer_prev).wait_send()

        @pl.when(e_prev)
        def _():
            r_copy(kp, peer_prev).wait_recv()
            r_forward(kp).start()
            RT[...] = RT[...] + recvR[kp]

        @pl.when(e_sib)
        def _():
            r_forward(kp).wait_recv()
            RT[...] = RT[...] + sibR[kp]

        @pl.when(e_prev)
        def _():
            r_forward(kp).wait_send()
            r_copy(kp, peer_prev).wait_send()

        @pl.when(k < levels)
        def _():
            va = dot(RT[:, 0:H], T2[0])
            VR[:, 0:H] = va
            VR[:, H:N] = dot(RT[:, H:N] - dot(va, G[...]), T2[1])
            sendR[...] = dot(VR[...], VX[...])

            @pl.when(e)
            def _():
                r_copy(k, peer).start()

        @pl.when((k == levels) & e_prev)
        def _():
            for p in range(3):
                q_copy(p, kp, peer_prev).wait_send()

        return d * 2

    lax.fori_loop(0, levels + 1, step, 1)

    va = dot(RT[own_rt, 0:H], T2[0])
    vb = dot(RT[own_rt, H:N] - dot(va, G[...]), T2[1])
    xb = dot(vb, T2[1], NN)
    out[:, H:N] = xb
    out[:, 0:H] = dot(va - dot(xb, G[...], NN), T2[0], NN)


def solution(mesh):
    slabs = mesh.shape["slab"]
    levels = (slabs - 1).bit_length()

    def on_device(coupling, tile_pattern, orbital_mass, sources):
        column = lax.axis_index("col")
        pattern = tile_pattern[0]
        mask = jnp.broadcast_to(
            pattern.T[:, None, :, None].astype(F32), (N // T // 2, T, N // T, T)
        ).reshape(H, N)
        rows = lax.broadcasted_iota(jnp.int32, (H, N), 0) + column * H
        cols = lax.broadcasted_iota(jnp.int32, (H, N), 1)
        brow = (rows == cols).astype(F32) + mask * coupling[0].T
        both = jnp.concatenate([orbital_mass[0], orbital_mass[0]])
        mine = (jnp.arange(N) // H == column).astype(F32)
        mrow = jnp.broadcast_to((both * mine)[None], (8, N))
        dma = pltpu.SemaphoreType.DMA
        vmem = pl.BlockSpec(memory_space=pltpu.VMEM)
        xt = pl.pallas_call(
            functools.partial(kernel, slabs, levels),
            out_shape=jax.ShapeDtypeStruct((T, N), F32),
            in_specs=[vmem] * 3,
            out_specs=vmem,
            scratch_shapes=[
                pltpu.VMEM((levels, N, N), F32),
                pltpu.VMEM((levels, 10, T, T), F32),
                pltpu.VMEM((levels, 10, T, T), F32),
                pltpu.VMEM((levels, M, N), F32),
                pltpu.VMEM((levels, M, N), F32),
                pltpu.VMEM((levels, N, N), F32),
                pltpu.VMEM((N, N), F32),
                pltpu.VMEM((N, N), F32),
                pltpu.VMEM((M, N), F32),
                pltpu.VMEM((M, N), F32),
                pltpu.VMEM((10, T, T), F32),
                pltpu.VMEM((10, T, T), F32),
                pltpu.VMEM((2, H, H), F32),
                pltpu.VMEM((H, H), F32),
                pltpu.VMEM((T, T), F32),
                pltpu.VMEM((18, 8, T), F32),
                pltpu.VMEM((8, N), F32),
                pltpu.VMEM((10, T, T), F32),
                pltpu.VMEM((N, N), F32),
                pltpu.VMEM((M, N), F32),
                dma((3,)),
                dma((3,)),
                dma((2,)),
                dma((2,)),
                dma((2,)),
                dma((2,)),
                dma((2,)),
                dma((levels, 2)),
                dma((3,)),
                dma((levels, 3)),
                dma((3,)),
                dma((levels, 3)),
                dma((2,)),
                dma((levels, 2)),
                dma(()),
                dma((levels,)),
                dma(()),
                dma((levels,)),
            ],
            compiler_params=pltpu.CompilerParams(
                collective_id=0, has_side_effects=True, vmem_limit_bytes=56 << 20
            ),
        )(brow, sources[0].T, mrow)
        return xt.T[None]

    placed = (
        P("slab", None, "col"),
        P("slab", None, "col"),
        P("slab", "col"),
        P("slab", None, "col"),
    )
    return jax.shard_map(
        on_device, mesh=mesh, in_specs=placed, out_specs=P("slab", None, "col"), check_vma=False
    )
```

```python
import functools

import jax
import jax.numpy as jnp
from jax import lax
from jax.experimental import pallas as pl
from jax.experimental.pallas import tpu as pltpu
from jax.sharding import PartitionSpec as P

F32 = jnp.float32
N = 512
H = 256
T = 128
M = 256
NT = (((1,), (1,)), ((), ()))
NN = (((1,), (0,)), ((), ()))
TILES = ((0, 0), (1, 0), (1, 1), (2, 0), (3, 0), (2, 1), (3, 1), (2, 2), (3, 2), (3, 3))
PIECES = ((0, 1), (1, 2), (3, 4), (7, 3))
MESH = pl.DeviceIdType.MESH


def dot(a, b, dims=NT):
    return lax.dot_general(
        a, b, dims, precision=lax.Precision.HIGHEST, preferred_element_type=F32
    )


def leaf(block, scr):
    rows = [block[8 * i : 8 * i + 8, :] for i in range(16)]
    lane = lax.broadcasted_iota(jnp.int32, (8, T), 1)
    sub = lax.broadcasted_iota(jnp.int32, (8, T), 0)
    out = []
    for J in range(16):
        b = (J % 2) * 9
        own = (lane >= 8 * J) & (lane < 8 * J + 8)
        for j in range(8):
            scr[b + j] = jnp.broadcast_to(rows[J][:, 8 * J + j : 8 * J + j + 1], (8, T))
        scr[b + 8] = jnp.where(own, jnp.where(lane == sub + 8 * J, 1.0, 0.0), rows[J])
        R = [jnp.broadcast_to(scr[b + 8, i : i + 1, :], (8, T)) for i in range(8)]
        E = [[None] * 8 for _ in range(8)]
        for i in range(8):
            for j in range(i + 1):
                E[i][j] = E[j][i] = jnp.broadcast_to(scr[b + j, i : i + 1, :], (8, T))
        V = [None] * 8
        for j in range(0, 8, 2):
            a, c, e = E[j][j], E[j][j + 1], E[j + 1][j + 1]
            q = 1.0 / (a * e - c * c)
            r = c * (1.0 / a)
            V[j] = R[j] * lax.rsqrt(a)
            V[j + 1] = (R[j + 1] - r * R[j]) * lax.rsqrt(e - c * r)
            ia, ic, ie = e * q, c * q, a * q
            R[j], R[j + 1] = ia * R[j] - ic * R[j + 1], ie * R[j + 1] - ic * R[j]
            for k in range(j + 2, 8):
                E[j][k], E[j + 1][k] = (
                    ia * E[j][k] - ic * E[j + 1][k],
                    ie * E[j + 1][k] - ic * E[j][k],
                )
            for i in range(8):
                if i in (j, j + 1):
                    continue
                m0, m1 = E[i][j], E[i][j + 1]
                R[i] = R[i] - (m0 * R[j] + m1 * R[j + 1])
                for k in range(j + 2, 8):
                    if i < j or k >= i:
                        E[i][k] = E[i][k] - (m0 * E[j][k] + m1 * E[j + 1][k])
            for i in range(j + 2, 8):
                for k in range(j + 2, i):
                    E[i][k] = E[k][i]
        for i in range(J + 1, 16):
            t = None
            for k in range(8):
                c = jnp.broadcast_to(rows[i][:, 8 * J + k : 8 * J + k + 1], (8, T)) * R[k]
                t = c if t is None else t + c
            rows[i] = jnp.where(own, 0.0, rows[i]) - t
        z = V[0]
        for r in range(1, 8):
            z = jnp.where(sub == r, V[r], z)
        out.append(jnp.where(lane <= sub + 8 * J, z, 0.0))
    return jnp.concatenate(out, 0)


def kernel(
    slabs,
    levels,
    brow,
    srct,
    mrow,
    out,
    recvP,
    recvQ,
    sibQ,
    recvR,
    sibR,
    VY,
    O,
    VX,
    VR,
    RT,
    D,
    DW,
    T2,
    G,
    W,
    scr,
    mb,
    sendQ,
    sendP,
    sendR,
    i_send,
    i_recv,
    n_send,
    n_recv,
    f_send,
    f_recv,
    v_send,
    v_recv,
    q_send,
    q_recv,
    qf_send,
    qf_recv,
    p_send,
    p_recv,
    r_send,
    r_recv,
    rf_send,
    rf_recv,
):
    s = lax.axis_index("slab")
    c = lax.axis_index("col")
    sgn = 2 * c - 1
    sib = 1 - c

    def inside(t):
        return (t >= 0) & (t < slabs)

    def remote(src, dst, ss, rs, slab, col):
        return pltpu.make_async_remote_copy(
            src_ref=src,
            dst_ref=dst,
            send_sem=ss,
            recv_sem=rs,
            device_id={"slab": slab, "col": col},
            device_id_type=MESH,
        )

    barrier = pltpu.get_barrier_semaphore()
    pl.semaphore_signal(barrier, inc=1, device_id={"slab": s, "col": sib}, device_id_type=MESH)
    count = 1
    for k in range(levels):
        peer = s + sgn * 2**k
        here = inside(peer)
        count = count + here.astype(jnp.int32)

        @pl.when(here)
        def _():
            pl.semaphore_signal(
                barrier, inc=1, device_id={"slab": peer, "col": sib}, device_id_type=MESH
            )

    pl.semaphore_wait(barrier, count)

    first = recvP.at[0]
    own_rt = pl.ds(pl.multiple_of(c * T, T), T)
    RT[own_rt, :] = srct[...]
    to_sib = functools.partial(remote, slab=s, col=sib)
    cp_m = to_sib(mrow, mb, i_send.at[0], i_recv.at[0])
    cp_r = to_sib(srct, RT.at[own_rt], i_send.at[1], i_recv.at[1])
    low, high, full = pl.ds(0, H), pl.ds(H, H), pl.ds(0, N)
    cp_b0 = to_sib(brow, first.at[low], i_send.at[2], i_recv.at[2])
    cp_b1 = to_sib(brow, O.at[high], i_send.at[2], i_recv.at[2])
    parts = ((low, low), (high, full), (low, high))
    nxt = [
        remote(first.at[p], first.at[p], n_send.at[i], n_recv.at[i], s + 1, 0)
        for i, p in enumerate(parts)
    ]
    fwd = [to_sib(first.at[p], O.at[p], f_send.at[i], f_recv.at[i]) for i, p in enumerate(parts[:2])]
    has_next, has_prior = s < slabs - 1, s > 0

    @pl.when(c == 0)
    def _():
        cp_b0.start()
        O[0:H, :] = brow[...]

        @pl.when(s == 0)
        def _():
            first[...] = jnp.zeros((N, N), F32)

    @pl.when(c == 1)
    def _():
        cp_b1.start()
        first[H:N, :] = brow[...]
        cp_b0.wait_recv()

        @pl.when(has_next)
        def _():
            for copy in nxt:
                copy.start()

        @pl.when(s == 0)
        def _():
            O[...] = jnp.zeros((N, N), F32)

    cp_m.start()
    cp_r.start()
    cp_m.wait()
    cp_r.wait()

    @pl.when(c == 0)
    def _():
        cp_b1.wait_recv()
        cp_b0.wait_send()

    @pl.when(c == 1)
    def _():
        cp_b1.wait_send()

    def arrive(part):
        @pl.when((c == 0) & has_prior)
        def _():
            nxt[part].wait_recv()
            fwd[part].start()

        @pl.when((c == 1) & has_prior)
        def _():
            fwd[part].wait_recv()

    eye = lax.broadcasted_iota(jnp.int32, (T, T), 0) == lax.broadcasted_iota(jnp.int32, (T, T), 1)

    def build(p):
        for n in range(PIECES[p][0], PIECES[p][0] + PIECES[p][1]):
            i, j = TILES[n]
            rr, cc = slice(T * i, T * i + T), slice(T * j, T * j + T)
            tile = first[rr, cc] + O[rr, cc]
            if i == j:
                mass = mrow[0:1, cc] + mb[0:1, cc]
                tile = tile + jnp.where(eye, jnp.broadcast_to(mass, (T, T)), 0.0)
            D[n] = tile

    def finish_first():
        @pl.when((c == 0) & has_prior)
        def _():
            nxt[2].wait_recv()
            fwd[0].wait_send()
            fwd[1].wait_send()

        @pl.when((c == 1) & has_next)
        def _():
            for copy in nxt:
                copy.wait_send()

        @pl.when((c == 1) & jnp.logical_not(has_next))
        def _():
            first[...] = jnp.zeros((N, N), F32)

    T2[...] = jnp.zeros((2, H, H), F32)

    def step(k, d):
        prev = d // 2
        e = inside(s + sgn * d) & (k < levels)
        e_prev = inside(s + sgn * prev) & (k >= 1)
        e_sib = inside(s - sgn * prev) & (k >= 1)
        kp = jnp.maximum(k - 1, 0)
        peer = s + sgn * d
        peer_prev = s + sgn * prev

        def q_copy(p, level, to):
            o, n = PIECES[p]
            return remote(
                sendQ.at[pl.ds(o, n)],
                recvQ.at[level, pl.ds(o, n)],
                q_send.at[p],
                q_recv.at[level, p],
                to,
                sib,
            )

        def q_forward(p, level):
            o, n = PIECES[p]
            return to_sib(
                recvQ.at[level, pl.ds(o, n)],
                sibQ.at[level, pl.ds(o, n)],
                qf_send.at[p],
                qf_recv.at[level, p],
            )

        def p_copy(h, level, to):
            rows = pl.ds(pl.multiple_of(h * H, H), H)
            return remote(
                sendP.at[rows],
                recvP.at[level + 1, rows],
                p_send.at[h],
                p_recv.at[level, h],
                to,
                sib,
            )

        def v_copy(h, level):
            rows = pl.ds(pl.multiple_of(h * H, H), H)
            return to_sib(VX.at[rows], VY.at[level, rows], v_send.at[h], v_recv.at[level, h])

        def r_copy(level, to):
            return remote(sendR, recvR.at[level], r_send, r_recv.at[level], to, sib)

        def r_forward(level):
            return to_sib(recvR.at[level], sibR.at[level], rf_send, rf_recv.at[level])

        def take(p):
            o, n = PIECES[p]

            @pl.when(k == 0)
            def _():
                if p in (0, 2):
                    arrive(p // 2)
                build(p)

            @pl.when(e_prev)
            def _():
                q_copy(p, kp, peer_prev).wait_recv()
                q_forward(p, kp).start()
                D[o : o + n] = D[o : o + n] - recvQ[kp, o : o + n]

            @pl.when(e_sib)
            def _():
                q_forward(p, kp).wait_recv()
                D[o : o + n] = D[o : o + n] - sibQ[kp, o : o + n]

            DW[o : o + n] = D[o : o + n]

            @pl.when(e_prev)
            def _():
                q_forward(p, kp).wait_send()

        take(0)

        def quarter(i, _):
            h = i // 2
            inv = leaf(DW[7 * h + 2 * (i - 2 * h)], scr)

            @pl.when(i == 0)
            def _():
                take(1)

            @pl.when(i == 2 * h)
            def _():
                T2[h, 0:T, 0:T] = inv
                g = dot(DW[7 * h + 1], inv)
                DW[7 * h + 2] = DW[7 * h + 2] - dot(g, g)
                W[...] = dot(g, inv, NN)

            @pl.when(i == 2 * h + 1)
            def _():
                T2[h, T:H, T:H] = inv
                T2[h, T:H, 0:T] = -dot(inv, W[...], NN)

            @pl.when(i == 1)
            def _():
                take(2)
                ba = jnp.concatenate(
                    [
                        jnp.concatenate([DW[3], DW[5]], 1),
                        jnp.concatenate([DW[4], DW[6]], 1),
                    ],
                    0,
                )
                g = dot(ba, T2[0])
                G[...] = g
                gg = dot(g, g)
                take(3)
                DW[7] = DW[7] - gg[0:T, 0:T]
                DW[8] = DW[8] - gg[T:H, 0:T]
                DW[9] = DW[9] - gg[T:H, T:H]

            return 0

        lax.fori_loop(0, 4, quarter, 0)

        @pl.when(k < levels)
        def _():
            @pl.when(k == 0)
            def _():
                finish_first()

            def solve(h):
                rows = slice(h * H, h * H + H)

                @pl.when(e_prev)
                def _():
                    p_copy(h, kp, peer_prev).wait_recv()

                @pl.when(k >= 1)
                def _():
                    v_copy(h, kp).wait_send()

                va = dot(recvP[k, rows, 0:H], T2[0])
                VX[rows, 0:H] = va
                VX[rows, H:N] = dot(recvP[k, rows, H:N] - dot(va, G[...]), T2[1])

                @pl.when(k < levels - 1)
                def _():
                    v_copy(h, k).start()

            def diagonal(i, j, pieces):
                qq = dot(VX[i * H : i * H + H, :], VX[j * H : j * H + H, :])
                for p in pieces:

                    @pl.when(e_prev)
                    def _():
                        q_copy(p, kp, peer_prev).wait_send()

                    for n in range(PIECES[p][0], PIECES[p][0] + PIECES[p][1]):
                        r0, c0 = TILES[n][0] * T - i * H, TILES[n][1] * T - j * H
                        sendQ[n] = qq[r0 : r0 + T, c0 : c0 + T]

                    @pl.when(e)
                    def _():
                        q_copy(p, k, peer).start()

            solve(0)
            diagonal(0, 0, (0, 1))
            solve(1)
            diagonal(1, 0, (2,))
            diagonal(1, 1, (3,))

        @pl.when(k < levels - 1)
        def _():
            def product(h, _):
                rows = pl.ds(pl.multiple_of(h * H, H), H)
                v_copy(h, k).wait_recv()

                @pl.when(e_prev)
                def _():
                    p_copy(h, kp, peer_prev).wait_send()

                sendP[rows, :] = dot(VY[k, rows, :], VX[...])

                @pl.when(e)
                def _():
                    p_copy(h, k, peer).start()

                @pl.when(jnp.logical_not(e))
                def _():
                    recvP[k + 1, rows, :] = jnp.zeros((H, N), F32)

                return 0

            lax.fori_loop(0, 2, product, 0)

        @pl.when((k == levels - 1) & e_prev)
        def _():
            p_copy(0, kp, peer_prev).wait_send()
            p_copy(1, kp, peer_prev).wait_send()

        @pl.when(e_prev)
        def _():
            r_copy(kp, peer_prev).wait_recv()
            r_forward(kp).start()
            RT[...] = RT[...] + recvR[kp]

        @pl.when(e_sib)
        def _():
            r_forward(kp).wait_recv()
            RT[...] = RT[...] + sibR[kp]

        @pl.when(e_prev)
        def _():
            r_forward(kp).wait_send()
            r_copy(kp, peer_prev).wait_send()

        @pl.when(k < levels)
        def _():
            va = dot(RT[:, 0:H], T2[0])
            VR[:, 0:H] = va
            VR[:, H:N] = dot(RT[:, H:N] - dot(va, G[...]), T2[1])
            sendR[...] = dot(VR[...], VX[...])

            @pl.when(e)
            def _():
                r_copy(k, peer).start()

        @pl.when((k == levels) & e_prev)
        def _():
            for p in range(len(PIECES)):
                q_copy(p, kp, peer_prev).wait_send()

        return d * 2

    lax.fori_loop(0, levels + 1, step, 1)

    va = dot(RT[own_rt, 0:H], T2[0])
    vb = dot(RT[own_rt, H:N] - dot(va, G[...]), T2[1])
    xb = dot(vb, T2[1], NN)
    out[:, H:N] = xb
    out[:, 0:H] = dot(va - dot(xb, G[...], NN), T2[0], NN)


def solution(mesh):
    slabs = mesh.shape["slab"]
    levels = (slabs - 1).bit_length()

    def on_device(coupling, tile_pattern, orbital_mass, sources):
        column = lax.axis_index("col")
        pattern = tile_pattern[0]
        mask = jnp.broadcast_to(
            pattern.T[:, None, :, None].astype(F32), (N // T // 2, T, N // T, T)
        ).reshape(H, N)
        rows = lax.broadcasted_iota(jnp.int32, (H, N), 0) + column * H
        cols = lax.broadcasted_iota(jnp.int32, (H, N), 1)
        brow = (rows == cols).astype(F32) + mask * coupling[0].T
        both = jnp.concatenate([orbital_mass[0], orbital_mass[0]])
        mine = (jnp.arange(N) // H == column).astype(F32)
        mrow = jnp.broadcast_to((both * mine)[None], (8, N))
        dma = pltpu.SemaphoreType.DMA
        vmem = pl.BlockSpec(memory_space=pltpu.VMEM)
        xt = pl.pallas_call(
            functools.partial(kernel, slabs, levels),
            out_shape=jax.ShapeDtypeStruct((T, N), F32),
            in_specs=[vmem] * 3,
            out_specs=vmem,
            scratch_shapes=[
                pltpu.VMEM((levels, N, N), F32),
                pltpu.VMEM((levels, 10, T, T), F32),
                pltpu.VMEM((levels, 10, T, T), F32),
                pltpu.VMEM((levels, M, N), F32),
                pltpu.VMEM((levels, M, N), F32),
                pltpu.VMEM((levels, N, N), F32),
                pltpu.VMEM((N, N), F32),
                pltpu.VMEM((N, N), F32),
                pltpu.VMEM((M, N), F32),
                pltpu.VMEM((M, N), F32),
                pltpu.VMEM((10, T, T), F32),
                pltpu.VMEM((10, T, T), F32),
                pltpu.VMEM((2, H, H), F32),
                pltpu.VMEM((H, H), F32),
                pltpu.VMEM((T, T), F32),
                pltpu.VMEM((18, 8, T), F32),
                pltpu.VMEM((8, N), F32),
                pltpu.VMEM((10, T, T), F32),
                pltpu.VMEM((N, N), F32),
                pltpu.VMEM((M, N), F32),
                dma((3,)),
                dma((3,)),
                dma((3,)),
                dma((3,)),
                dma((2,)),
                dma((2,)),
                dma((2,)),
                dma((levels, 2)),
                dma((len(PIECES),)),
                dma((levels, len(PIECES))),
                dma((len(PIECES),)),
                dma((levels, len(PIECES))),
                dma((2,)),
                dma((levels, 2)),
                dma(()),
                dma((levels,)),
                dma(()),
                dma((levels,)),
            ],
            compiler_params=pltpu.CompilerParams(
                collective_id=0, has_side_effects=True, vmem_limit_bytes=56 << 20
            ),
        )(brow, sources[0].T, mrow)
        return xt.T[None]

    placed = (
        P("slab", None, "col"),
        P("slab", None, "col"),
        P("slab", "col"),
        P("slab", None, "col"),
    )
    return jax.shard_map(
        on_device, mesh=mesh, in_specs=placed, out_specs=P("slab", None, "col"), check_vma=False
    )
```

```python
import functools

import jax
import jax.numpy as jnp
from jax import lax
from jax.experimental import pallas as pl
from jax.experimental.pallas import tpu as pltpu
from jax.sharding import PartitionSpec as P

F32 = jnp.float32
N = 512
H = 256
T = 128
M = 256
NT = (((1,), (1,)), ((), ()))
NN = (((1,), (0,)), ((), ()))
TILES = ((0, 0), (1, 0), (1, 1), (2, 0), (3, 0), (2, 1), (3, 1), (2, 2), (3, 2), (3, 3))
PIECES = ((0, 1), (1, 2), (3, 4), (7, 3))
MESH = pl.DeviceIdType.MESH


def dot(a, b, dims=NT):
    return lax.dot_general(
        a, b, dims, precision=lax.Precision.HIGHEST, preferred_element_type=F32
    )


def leaf(block, scr):
    rows = [block[8 * i : 8 * i + 8, :] for i in range(16)]
    lane = lax.broadcasted_iota(jnp.int32, (8, T), 1)
    sub = lax.broadcasted_iota(jnp.int32, (8, T), 0)
    out = []
    for J in range(16):
        b = (J % 2) * 9
        own = (lane >= 8 * J) & (lane < 8 * J + 8)
        for j in range(8):
            scr[b + j] = jnp.broadcast_to(rows[J][:, 8 * J + j : 8 * J + j + 1], (8, T))
        scr[b + 8] = jnp.where(own, jnp.where(lane == sub + 8 * J, 1.0, 0.0), rows[J])
        R = [jnp.broadcast_to(scr[b + 8, i : i + 1, :], (8, T)) for i in range(8)]
        E = [[None] * 8 for _ in range(8)]
        for i in range(8):
            for j in range(i + 1):
                E[i][j] = E[j][i] = jnp.broadcast_to(scr[b + j, i : i + 1, :], (8, T))
        V = [None] * 8
        for j in range(0, 8, 2):
            a, c, e = E[j][j], E[j][j + 1], E[j + 1][j + 1]
            q = 1.0 / (a * e - c * c)
            r = c * (1.0 / a)
            V[j] = R[j] * lax.rsqrt(a)
            V[j + 1] = (R[j + 1] - r * R[j]) * lax.rsqrt(e - c * r)
            ia, ic, ie = e * q, c * q, a * q
            R[j], R[j + 1] = ia * R[j] - ic * R[j + 1], ie * R[j + 1] - ic * R[j]
            for k in range(j + 2, 8):
                E[j][k], E[j + 1][k] = (
                    ia * E[j][k] - ic * E[j + 1][k],
                    ie * E[j + 1][k] - ic * E[j][k],
                )
            for i in range(8):
                if i in (j, j + 1):
                    continue
                m0, m1 = E[i][j], E[i][j + 1]
                R[i] = R[i] - (m0 * R[j] + m1 * R[j + 1])
                for k in range(j + 2, 8):
                    if i < j or k >= i:
                        E[i][k] = E[i][k] - (m0 * E[j][k] + m1 * E[j + 1][k])
            for i in range(j + 2, 8):
                for k in range(j + 2, i):
                    E[i][k] = E[k][i]
        for i in range(J + 1, 16):
            t = None
            for k in range(8):
                c = jnp.broadcast_to(rows[i][:, 8 * J + k : 8 * J + k + 1], (8, T)) * R[k]
                t = c if t is None else t + c
            rows[i] = jnp.where(own, 0.0, rows[i]) - t
        z = V[0]
        for r in range(1, 8):
            z = jnp.where(sub == r, V[r], z)
        out.append(jnp.where(lane <= sub + 8 * J, z, 0.0))
    return jnp.concatenate(out, 0)


def kernel(
    slabs,
    levels,
    brow,
    srct,
    mrow,
    out,
    recvP,
    recvQ,
    sibQ,
    recvR,
    sibR,
    VY,
    O,
    VX,
    VR,
    RT,
    D,
    DW,
    T2,
    G,
    W,
    scr,
    mb,
    sendQ,
    sendP,
    sendR,
    xrecv,
    xsum,
    i_send,
    i_recv,
    n_send,
    n_recv,
    f_send,
    f_recv,
    v_send,
    v_recv,
    q_send,
    q_recv,
    qf_send,
    qf_recv,
    p_send,
    p_recv,
    r_send,
    r_recv,
    rf_send,
    rf_recv,
    x_send,
    x_recv,
):
    s = lax.axis_index("slab")
    c = lax.axis_index("col")
    sgn = 2 * c - 1
    sib = 1 - c

    eliminating = tuple(range(1, levels - 1, 2))

    def inside(t):
        return (t >= 0) & (t < slabs)

    def eliminates(k):
        return (k % 2 == 1) & (k < levels - 1)

    def odd(t, d):
        return ((t + slabs) // d) % 2 == 1

    own_level = levels
    for k in reversed(eliminating):
        own_level = jnp.where(odd(s, 2**k), k, own_level)

    def remote(src, dst, ss, rs, slab, col):
        return pltpu.make_async_remote_copy(
            src_ref=src,
            dst_ref=dst,
            send_sem=ss,
            recv_sem=rs,
            device_id={"slab": slab, "col": col},
            device_id_type=MESH,
        )

    barrier = pltpu.get_barrier_semaphore()
    pl.semaphore_signal(barrier, inc=1, device_id={"slab": s, "col": sib}, device_id_type=MESH)
    count = 1
    for k in range(levels):
        peer = s + sgn * 2**k
        here = inside(peer)
        count = count + here.astype(jnp.int32)

        @pl.when(here)
        def _():
            pl.semaphore_signal(
                barrier, inc=1, device_id={"slab": peer, "col": sib}, device_id_type=MESH
            )

    for k in eliminating:
        for peer in (s - 2**k, s + 2**k):
            here = inside(peer)
            count = count + here.astype(jnp.int32)

            @pl.when(here)
            def _():
                pl.semaphore_signal(
                    barrier, inc=1, device_id={"slab": peer, "col": c}, device_id_type=MESH
                )

    pl.semaphore_wait(barrier, count)

    first = recvP.at[0]
    own_rt = pl.ds(pl.multiple_of(c * T, T), T)
    RT[own_rt, :] = srct[...]
    to_sib = functools.partial(remote, slab=s, col=sib)
    cp_m = to_sib(mrow, mb, i_send.at[0], i_recv.at[0])
    cp_r = to_sib(srct, RT.at[own_rt], i_send.at[1], i_recv.at[1])
    low, high, full = pl.ds(0, H), pl.ds(H, H), pl.ds(0, N)
    cp_b0 = to_sib(brow, first.at[low], i_send.at[2], i_recv.at[2])
    cp_b1 = to_sib(brow, O.at[high], i_send.at[2], i_recv.at[2])
    parts = ((low, low), (high, full), (low, high))
    nxt = [
        remote(first.at[p], first.at[p], n_send.at[i], n_recv.at[i], s + 1, 0)
        for i, p in enumerate(parts)
    ]
    fwd = [to_sib(first.at[p], O.at[p], f_send.at[i], f_recv.at[i]) for i, p in enumerate(parts[:2])]
    has_next, has_prior = s < slabs - 1, s > 0

    @pl.when(c == 0)
    def _():
        cp_b0.start()
        O[0:H, :] = brow[...]

        @pl.when(s == 0)
        def _():
            first[...] = jnp.zeros((N, N), F32)

    @pl.when(c == 1)
    def _():
        cp_b1.start()
        first[H:N, :] = brow[...]
        cp_b0.wait_recv()

        @pl.when(has_next)
        def _():
            for copy in nxt:
                copy.start()

        @pl.when(s == 0)
        def _():
            O[...] = jnp.zeros((N, N), F32)

    cp_m.start()
    cp_r.start()
    cp_m.wait()
    cp_r.wait()

    @pl.when(c == 0)
    def _():
        cp_b1.wait_recv()
        cp_b0.wait_send()

    @pl.when(c == 1)
    def _():
        cp_b1.wait_send()

    def arrive(part):
        @pl.when((c == 0) & has_prior)
        def _():
            nxt[part].wait_recv()
            fwd[part].start()

        @pl.when((c == 1) & has_prior)
        def _():
            fwd[part].wait_recv()

    eye = lax.broadcasted_iota(jnp.int32, (T, T), 0) == lax.broadcasted_iota(jnp.int32, (T, T), 1)

    def build(p):
        for n in range(PIECES[p][0], PIECES[p][0] + PIECES[p][1]):
            i, j = TILES[n]
            rr, cc = slice(T * i, T * i + T), slice(T * j, T * j + T)
            tile = first[rr, cc] + O[rr, cc]
            if i == j:
                mass = mrow[0:1, cc] + mb[0:1, cc]
                tile = tile + jnp.where(eye, jnp.broadcast_to(mass, (T, T)), 0.0)
            D[n] = tile

    def finish_first():
        @pl.when((c == 0) & has_prior)
        def _():
            nxt[2].wait_recv()
            fwd[0].wait_send()
            fwd[1].wait_send()

        @pl.when((c == 1) & has_next)
        def _():
            for copy in nxt:
                copy.wait_send()

        @pl.when((c == 1) & jnp.logical_not(has_next))
        def _():
            first[...] = jnp.zeros((N, N), F32)

    T2[...] = jnp.zeros((2, H, H), F32)

    def step(k, d):
        prev = d // 2
        kp = jnp.maximum(k - 1, 0)
        peer = s + sgn * d
        peer_prev = s + sgn * prev
        alive = k <= own_level
        work = alive & jnp.logical_not(eliminates(k) & (own_level != k))
        work_prev = (k >= 1) & (kp <= own_level) & jnp.logical_not(eliminates(kp) & (own_level != kp))
        rx = (k >= 1) & alive & inside(peer_prev)
        rx_sib = (k >= 1) & alive & inside(s - sgn * prev)
        rx_p = rx & (k < levels) & (jnp.logical_not(eliminates(k)) | (own_level == k))
        tx = work & (k < levels) & inside(peer)
        tx_p = tx & (k < levels - 1) & (jnp.logical_not(eliminates(k + 1)) | odd(peer, 2 * d))
        tx_prev = work_prev & inside(peer_prev)
        tx_p_prev = tx_prev & (k < levels) & (jnp.logical_not(eliminates(k)) | odd(peer_prev, d))
        tx_v_prev = work_prev & (k < levels)

        def q_copy(p, level, to):
            o, n = PIECES[p]
            return remote(
                sendQ.at[pl.ds(o, n)],
                recvQ.at[level, pl.ds(o, n)],
                q_send.at[p],
                q_recv.at[level, p],
                to,
                sib,
            )

        def q_forward(p, level):
            o, n = PIECES[p]
            return to_sib(
                recvQ.at[level, pl.ds(o, n)],
                sibQ.at[level, pl.ds(o, n)],
                qf_send.at[p],
                qf_recv.at[level, p],
            )

        def p_copy(h, level, to):
            rows = pl.ds(pl.multiple_of(h * H, H), H)
            return remote(
                sendP.at[rows],
                recvP.at[level + 1, rows],
                p_send.at[h],
                p_recv.at[level, h],
                to,
                sib,
            )

        def v_copy(h, level):
            rows = pl.ds(pl.multiple_of(h * H, H), H)
            return to_sib(VX.at[rows], VY.at[level, rows], v_send.at[h], v_recv.at[level, h])

        def r_copy(level, to):
            return remote(sendR, recvR.at[level], r_send, r_recv.at[level], to, sib)

        def r_forward(level):
            return to_sib(recvR.at[level], sibR.at[level], rf_send, rf_recv.at[level])

        def sent_q(p):
            @pl.when(tx_prev)
            def _():
                q_copy(p, kp, peer_prev).wait_send()

        def sent_p(h):
            @pl.when(tx_p_prev)
            def _():
                p_copy(h, kp, peer_prev).wait_send()

        def sent_v(h):
            @pl.when(tx_v_prev)
            def _():
                v_copy(h, kp).wait_send()

        def sent_r():
            @pl.when(tx_prev)
            def _():
                r_copy(kp, peer_prev).wait_send()

        def take(p):
            o, n = PIECES[p]

            @pl.when(k == 0)
            def _():
                if p in (0, 2):
                    arrive(p // 2)
                build(p)

            @pl.when(rx)
            def _():
                q_copy(p, kp, peer_prev).wait_recv()
                q_forward(p, kp).start()
                D[o : o + n] = D[o : o + n] - recvQ[kp, o : o + n]

            @pl.when(rx_sib)
            def _():
                q_forward(p, kp).wait_recv()
                D[o : o + n] = D[o : o + n] - sibQ[kp, o : o + n]

            DW[o : o + n] = D[o : o + n]

            @pl.when(rx)
            def _():
                q_forward(p, kp).wait_send()

        def quarter(i, _):
            h = i // 2
            inv = leaf(DW[7 * h + 2 * (i - 2 * h)], scr)

            @pl.when(i == 0)
            def _():
                take(1)

            @pl.when(i == 2 * h)
            def _():
                T2[h, 0:T, 0:T] = inv
                g = dot(DW[7 * h + 1], inv)
                DW[7 * h + 2] = DW[7 * h + 2] - dot(g, g)
                W[...] = dot(g, inv, NN)

            @pl.when(i == 2 * h + 1)
            def _():
                T2[h, T:H, T:H] = inv
                T2[h, T:H, 0:T] = -dot(inv, W[...], NN)

            @pl.when(i == 1)
            def _():
                take(2)
                ba = jnp.concatenate(
                    [
                        jnp.concatenate([DW[3], DW[5]], 1),
                        jnp.concatenate([DW[4], DW[6]], 1),
                    ],
                    0,
                )
                g = dot(ba, T2[0])
                G[...] = g
                gg = dot(g, g)
                take(3)
                DW[7] = DW[7] - gg[0:T, 0:T]
                DW[8] = DW[8] - gg[T:H, 0:T]
                DW[9] = DW[9] - gg[T:H, T:H]

            return 0

        @pl.when(work)
        def _():
            take(0)
            lax.fori_loop(0, 4, quarter, 0)

        @pl.when(alive & jnp.logical_not(work))
        def _():
            for p in range(len(PIECES)):
                take(p)

        @pl.when(work & (k < levels))
        def _():
            @pl.when(k == 0)
            def _():
                finish_first()

            @pl.when((k >= 1) & jnp.logical_not(inside(peer_prev)))
            def _():
                recvP[k] = jnp.zeros((N, N), F32)

            def solve(h):
                rows = slice(h * H, h * H + H)

                @pl.when(rx_p)
                def _():
                    p_copy(h, kp, peer_prev).wait_recv()

                sent_v(h)
                va = dot(recvP[k, rows, 0:H], T2[0])
                VX[rows, 0:H] = va
                VX[rows, H:N] = dot(recvP[k, rows, H:N] - dot(va, G[...]), T2[1])

                @pl.when(k < levels - 1)
                def _():
                    v_copy(h, k).start()

            def diagonal(i, j, pieces):
                qq = dot(VX[i * H : i * H + H, :], VX[j * H : j * H + H, :])
                for p in pieces:
                    sent_q(p)
                    for n in range(PIECES[p][0], PIECES[p][0] + PIECES[p][1]):
                        r0, c0 = TILES[n][0] * T - i * H, TILES[n][1] * T - j * H
                        sendQ[n] = qq[r0 : r0 + T, c0 : c0 + T]

                    @pl.when(tx)
                    def _():
                        q_copy(p, k, peer).start()

            solve(0)
            diagonal(0, 0, (0, 1))
            solve(1)
            diagonal(1, 0, (2,))
            diagonal(1, 1, (3,))

            def product(h, _):
                rows = pl.ds(pl.multiple_of(h * H, H), H)
                sent_p(h)

                @pl.when(k < levels - 1)
                def _():
                    v_copy(h, k).wait_recv()

                @pl.when(tx_p)
                def _():
                    sendP[rows, :] = dot(VY[k, rows, :], VX[...])
                    p_copy(h, k, peer).start()

                return 0

            lax.fori_loop(0, 2, product, 0)

        @pl.when(rx)
        def _():
            r_copy(kp, peer_prev).wait_recv()
            r_forward(kp).start()
            RT[...] = RT[...] + recvR[kp]

        @pl.when(rx_sib)
        def _():
            r_forward(kp).wait_recv()
            RT[...] = RT[...] + sibR[kp]

        @pl.when(rx)
        def _():
            r_forward(kp).wait_send()

        sent_r()

        @pl.when(work & (k < levels))
        def _():
            va = dot(RT[:, 0:H], T2[0])
            VR[:, 0:H] = va
            VR[:, H:N] = dot(RT[:, H:N] - dot(va, G[...]), T2[1])
            sendR[...] = dot(VR[...], VX[...])

            @pl.when(tx)
            def _():
                r_copy(k, peer).start()

        @pl.when(jnp.logical_not(work & (k < levels)))
        def _():
            for p in range(len(PIECES)):
                sent_q(p)
            for h in range(2):
                sent_p(h)
                sent_v(h)

        return d * 2

    lax.fori_loop(0, levels + 1, step, 1)

    def backward(va, vb):
        xb = dot(vb, T2[1], NN)
        out[:, H:N] = xb
        out[:, 0:H] = dot(va - dot(xb, G[...], NN), T2[0], NN)

    @pl.when(own_level == levels)
    def _():
        va = dot(RT[own_rt, 0:H], T2[0])
        backward(va, dot(RT[own_rt, H:N] - dot(va, G[...]), T2[1]))

    for n, k in enumerate(reversed(eliminating)):
        d = 2**k
        ways = (s - sgn * d, s + sgn * d)

        def x_copy(way):
            return remote(out, xrecv.at[way], x_send.at[n, way], x_recv.at[way], ways[way], c)

        for way in range(2):

            @pl.when((own_level > k) & inside(ways[way]))
            def _():
                x_copy(way).start()

        @pl.when(own_level == k)
        def _():
            xsum[...] = VR[own_rt, :]

            @pl.when(inside(ways[1]))
            def _():
                x_copy(0).wait_recv()
                xsum[...] = xsum[...] + dot(xrecv[0], VX[...], NN)

            @pl.when(inside(ways[0]))
            def _():
                x_copy(1).wait_recv()
                xsum[...] = xsum[...] + dot(xrecv[1], VY[k], NN)

            backward(xsum[:, 0:H], xsum[:, H:N])

    for n, k in enumerate(reversed(eliminating)):
        d = 2**k
        ways = (s - sgn * d, s + sgn * d)
        for way in range(2):

            @pl.when((own_level > k) & inside(ways[way]))
            def _():
                remote(
                    out, xrecv.at[way], x_send.at[n, way], x_recv.at[way], ways[way], c
                ).wait_send()


def solution(mesh):
    slabs = mesh.shape["slab"]
    levels = (slabs - 1).bit_length()

    def on_device(coupling, tile_pattern, orbital_mass, sources):
        column = lax.axis_index("col")
        pattern = tile_pattern[0]
        mask = jnp.broadcast_to(
            pattern.T[:, None, :, None].astype(F32), (N // T // 2, T, N // T, T)
        ).reshape(H, N)
        rows = lax.broadcasted_iota(jnp.int32, (H, N), 0) + column * H
        cols = lax.broadcasted_iota(jnp.int32, (H, N), 1)
        brow = (rows == cols).astype(F32) + mask * coupling[0].T
        both = jnp.concatenate([orbital_mass[0], orbital_mass[0]])
        mine = (jnp.arange(N) // H == column).astype(F32)
        mrow = jnp.broadcast_to((both * mine)[None], (8, N))
        dma = pltpu.SemaphoreType.DMA
        vmem = pl.BlockSpec(memory_space=pltpu.VMEM)
        xt = pl.pallas_call(
            functools.partial(kernel, slabs, levels),
            out_shape=jax.ShapeDtypeStruct((T, N), F32),
            in_specs=[vmem] * 3,
            out_specs=vmem,
            scratch_shapes=[
                pltpu.VMEM((levels, N, N), F32),
                pltpu.VMEM((levels, 10, T, T), F32),
                pltpu.VMEM((levels, 10, T, T), F32),
                pltpu.VMEM((levels, M, N), F32),
                pltpu.VMEM((levels, M, N), F32),
                pltpu.VMEM((levels, N, N), F32),
                pltpu.VMEM((N, N), F32),
                pltpu.VMEM((N, N), F32),
                pltpu.VMEM((M, N), F32),
                pltpu.VMEM((M, N), F32),
                pltpu.VMEM((10, T, T), F32),
                pltpu.VMEM((10, T, T), F32),
                pltpu.VMEM((2, H, H), F32),
                pltpu.VMEM((H, H), F32),
                pltpu.VMEM((T, T), F32),
                pltpu.VMEM((18, 8, T), F32),
                pltpu.VMEM((8, N), F32),
                pltpu.VMEM((10, T, T), F32),
                pltpu.VMEM((N, N), F32),
                pltpu.VMEM((M, N), F32),
                pltpu.VMEM((2, T, N), F32),
                pltpu.VMEM((T, N), F32),
                dma((3,)),
                dma((3,)),
                dma((3,)),
                dma((3,)),
                dma((2,)),
                dma((2,)),
                dma((2,)),
                dma((levels, 2)),
                dma((len(PIECES),)),
                dma((levels, len(PIECES))),
                dma((len(PIECES),)),
                dma((levels, len(PIECES))),
                dma((2,)),
                dma((levels, 2)),
                dma(()),
                dma((levels,)),
                dma(()),
                dma((levels,)),
                dma((levels, 2)),
                dma((2,)),
            ],
            compiler_params=pltpu.CompilerParams(
                collective_id=0, has_side_effects=True, vmem_limit_bytes=56 << 20
            ),
        )(brow, sources[0].T, mrow)
        return xt.T[None]

    placed = (
        P("slab", None, "col"),
        P("slab", None, "col"),
        P("slab", "col"),
        P("slab", None, "col"),
    )
    return jax.shard_map(
        on_device, mesh=mesh, in_specs=placed, out_specs=P("slab", None, "col"), check_vma=False
    )
```

```python
import functools

import jax
import jax.numpy as jnp
from jax import lax
from jax.experimental import pallas as pl
from jax.experimental.pallas import tpu as pltpu
from jax.sharding import PartitionSpec as P

F32 = jnp.float32
N = 512
H = 256
T = 128
M = 256
NT = (((1,), (1,)), ((), ()))
NN = (((1,), (0,)), ((), ()))
TILES = ((0, 0), (1, 0), (1, 1), (2, 0), (3, 0), (2, 1), (3, 1), (2, 2), (3, 2), (3, 3))
PIECES = ((0, 1), (1, 2), (3, 4), (7, 3))
MESH = pl.DeviceIdType.MESH


def dot(a, b, dims=NT):
    return lax.dot_general(
        a, b, dims, precision=lax.Precision.HIGHEST, preferred_element_type=F32
    )


def leaf(block, scr):
    rows = [block[8 * i : 8 * i + 8, :] for i in range(16)]
    lane = lax.broadcasted_iota(jnp.int32, (8, T), 1)
    sub = lax.broadcasted_iota(jnp.int32, (8, T), 0)
    out = []
    for J in range(16):
        b = (J % 2) * 9
        own = (lane >= 8 * J) & (lane < 8 * J + 8)
        for j in range(8):
            scr[b + j] = jnp.broadcast_to(rows[J][:, 8 * J + j : 8 * J + j + 1], (8, T))
        scr[b + 8] = jnp.where(own, jnp.where(lane == sub + 8 * J, 1.0, 0.0), rows[J])
        R = [jnp.broadcast_to(scr[b + 8, i : i + 1, :], (8, T)) for i in range(8)]
        E = [[None] * 8 for _ in range(8)]
        for i in range(8):
            for j in range(i + 1):
                E[i][j] = E[j][i] = jnp.broadcast_to(scr[b + j, i : i + 1, :], (8, T))
        V = [None] * 8
        for j in range(0, 8, 2):
            a, c, e = E[j][j], E[j][j + 1], E[j + 1][j + 1]
            q = 1.0 / (a * e - c * c)
            r = c * (1.0 / a)
            V[j] = R[j] * lax.rsqrt(a)
            V[j + 1] = (R[j + 1] - r * R[j]) * lax.rsqrt(e - c * r)
            ia, ic, ie = e * q, c * q, a * q
            R[j], R[j + 1] = ia * R[j] - ic * R[j + 1], ie * R[j + 1] - ic * R[j]
            for k in range(j + 2, 8):
                E[j][k], E[j + 1][k] = (
                    ia * E[j][k] - ic * E[j + 1][k],
                    ie * E[j + 1][k] - ic * E[j][k],
                )
            for i in range(8):
                if i in (j, j + 1):
                    continue
                m0, m1 = E[i][j], E[i][j + 1]
                R[i] = R[i] - (m0 * R[j] + m1 * R[j + 1])
                for k in range(j + 2, 8):
                    if i < j or k >= i:
                        E[i][k] = E[i][k] - (m0 * E[j][k] + m1 * E[j + 1][k])
            for i in range(j + 2, 8):
                for k in range(j + 2, i):
                    E[i][k] = E[k][i]
        for i in range(J + 1, 16):
            t = None
            for k in range(8):
                c = jnp.broadcast_to(rows[i][:, 8 * J + k : 8 * J + k + 1], (8, T)) * R[k]
                t = c if t is None else t + c
            rows[i] = jnp.where(own, 0.0, rows[i]) - t
        z = V[0]
        for r in range(1, 8):
            z = jnp.where(sub == r, V[r], z)
        out.append(jnp.where(lane <= sub + 8 * J, z, 0.0))
    return jnp.concatenate(out, 0)


def kernel(
    slabs,
    levels,
    brow,
    src,
    mrow,
    out,
    recvP,
    recvQ,
    sibQ,
    recvR,
    sibR,
    VY,
    O,
    VX,
    VR,
    RT,
    D,
    DW,
    T2,
    G,
    W,
    scr,
    mb,
    sendQ,
    sendP,
    sendR,
    i_send,
    i_recv,
    n_send,
    n_recv,
    f_send,
    f_recv,
    v_send,
    v_recv,
    q_send,
    q_recv,
    qf_send,
    qf_recv,
    p_send,
    p_recv,
    r_send,
    r_recv,
    rf_send,
    rf_recv,
):
    s = lax.axis_index("slab")
    c = lax.axis_index("col")
    sgn = 2 * c - 1
    sib = 1 - c

    def inside(t):
        return (t >= 0) & (t < slabs)

    def remote(src, dst, ss, rs, slab, col):
        return pltpu.make_async_remote_copy(
            src_ref=src,
            dst_ref=dst,
            send_sem=ss,
            recv_sem=rs,
            device_id={"slab": slab, "col": col},
            device_id_type=MESH,
        )

    barrier = pltpu.get_barrier_semaphore()
    pl.semaphore_signal(barrier, inc=1, device_id={"slab": s, "col": sib}, device_id_type=MESH)
    count = 1
    for k in range(levels):
        peer = s + sgn * 2**k
        here = inside(peer)
        count = count + here.astype(jnp.int32)

        @pl.when(here)
        def _():
            pl.semaphore_signal(
                barrier, inc=1, device_id={"slab": peer, "col": sib}, device_id_type=MESH
            )

    pl.semaphore_wait(barrier, count)

    first = recvP.at[0]
    own_rt = pl.ds(pl.multiple_of(c * T, T), T)
    RT[own_rt, :] = src[...].T
    to_sib = functools.partial(remote, slab=s, col=sib)
    cp_m = to_sib(mrow, mb, i_send.at[0], i_recv.at[0])
    cp_r = to_sib(RT.at[own_rt], RT.at[own_rt], i_send.at[1], i_recv.at[1])
    low, high, full = pl.ds(0, H), pl.ds(H, H), pl.ds(0, N)
    cp_b0 = to_sib(brow, first.at[low], i_send.at[2], i_recv.at[2])
    cp_b1 = to_sib(brow, O.at[high], i_send.at[2], i_recv.at[2])
    parts = ((low, low), (high, full), (low, high))
    nxt = [
        remote(first.at[p], first.at[p], n_send.at[i], n_recv.at[i], s + 1, 0)
        for i, p in enumerate(parts)
    ]
    fwd = [to_sib(first.at[p], O.at[p], f_send.at[i], f_recv.at[i]) for i, p in enumerate(parts[:2])]
    has_next, has_prior = s < slabs - 1, s > 0

    @pl.when(c == 0)
    def _():
        cp_b0.start()
        O[0:H, :] = brow[...]

        @pl.when(s == 0)
        def _():
            first[...] = jnp.zeros((N, N), F32)

    @pl.when(c == 1)
    def _():
        cp_b1.start()
        first[H:N, :] = brow[...]
        cp_b0.wait_recv()

        @pl.when(has_next)
        def _():
            for copy in nxt:
                copy.start()

        @pl.when(s == 0)
        def _():
            O[...] = jnp.zeros((N, N), F32)

    cp_m.start()
    cp_r.start()
    cp_m.wait()
    cp_r.wait()

    @pl.when(c == 0)
    def _():
        cp_b1.wait_recv()
        cp_b0.wait_send()

    @pl.when(c == 1)
    def _():
        cp_b1.wait_send()

    def arrive(part):
        @pl.when((c == 0) & has_prior)
        def _():
            nxt[part].wait_recv()
            fwd[part].start()

        @pl.when((c == 1) & has_prior)
        def _():
            fwd[part].wait_recv()

    eye = lax.broadcasted_iota(jnp.int32, (T, T), 0) == lax.broadcasted_iota(jnp.int32, (T, T), 1)

    def build(p):
        for n in range(PIECES[p][0], PIECES[p][0] + PIECES[p][1]):
            i, j = TILES[n]
            rr, cc = slice(T * i, T * i + T), slice(T * j, T * j + T)
            tile = first[rr, cc] + O[rr, cc]
            if i == j:
                mass = mrow[0:1, cc] + mb[0:1, cc]
                tile = tile + jnp.where(eye, jnp.broadcast_to(mass, (T, T)), 0.0)
            D[n] = tile

    def finish_first():
        @pl.when((c == 0) & has_prior)
        def _():
            nxt[2].wait_recv()
            fwd[0].wait_send()
            fwd[1].wait_send()

        @pl.when((c == 1) & has_next)
        def _():
            for copy in nxt:
                copy.wait_send()

        @pl.when((c == 1) & jnp.logical_not(has_next))
        def _():
            first[...] = jnp.zeros((N, N), F32)

    T2[...] = jnp.zeros((2, 2, H, H), F32)

    def step(k, d):
        prev = d // 2
        slot, was = k % 2, (k + 1) % 2
        e = inside(s + sgn * d) & (k < levels)
        e_prev = inside(s + sgn * prev) & (k >= 1)
        e_sib = inside(s - sgn * prev) & (k >= 1)
        kp = jnp.maximum(k - 1, 0)
        peer = s + sgn * d
        peer_prev = s + sgn * prev

        def q_copy(p, level, to):
            o, n = PIECES[p]
            return remote(
                sendQ.at[pl.ds(o, n)],
                recvQ.at[level, pl.ds(o, n)],
                q_send.at[p],
                q_recv.at[level, p],
                to,
                sib,
            )

        def q_forward(p, level):
            o, n = PIECES[p]
            return to_sib(
                recvQ.at[level, pl.ds(o, n)],
                sibQ.at[level, pl.ds(o, n)],
                qf_send.at[p],
                qf_recv.at[level, p],
            )

        def p_copy(h, level, to):
            rows = pl.ds(pl.multiple_of(h * H, H), H)
            return remote(
                sendP.at[rows],
                recvP.at[level + 1, rows],
                p_send.at[h],
                p_recv.at[level, h],
                to,
                sib,
            )

        def v_copy(h, level):
            rows = pl.ds(pl.multiple_of(h * H, H), H)
            return to_sib(VX.at[rows], VY.at[level, rows], v_send.at[h], v_recv.at[level, h])

        def r_copy(level, to):
            return remote(sendR, recvR.at[level], r_send, r_recv.at[level], to, sib)

        def r_forward(level):
            return to_sib(recvR.at[level], sibR.at[level], rf_send, rf_recv.at[level])

        def take(p):
            o, n = PIECES[p]

            @pl.when(k == 0)
            def _():
                if p in (0, 2):
                    arrive(p // 2)
                build(p)

            @pl.when(e_prev)
            def _():
                q_copy(p, kp, peer_prev).wait_recv()
                q_forward(p, kp).start()
                D[o : o + n] = D[o : o + n] - recvQ[kp, o : o + n]

            @pl.when(e_sib)
            def _():
                q_forward(p, kp).wait_recv()
                D[o : o + n] = D[o : o + n] - sibQ[kp, o : o + n]

            DW[o : o + n] = D[o : o + n]

            @pl.when(e_prev)
            def _():
                q_forward(p, kp).wait_send()

        take(0)

        def take_rhs(level, stride, on):
            there = s + sgn * stride

            @pl.when(on & inside(there))
            def _():
                r_copy(level, there).wait_recv()
                r_forward(level).start()
                RT[...] = RT[...] + recvR[level]

            @pl.when(on & inside(s - sgn * stride))
            def _():
                r_forward(level).wait_recv()
                RT[...] = RT[...] + sibR[level]

            @pl.when(on & inside(there))
            def _():
                r_forward(level).wait_send()
                r_copy(level, there).wait_send()

        def rhs():
            take_rhs(jnp.maximum(k - 2, 0), d // 4, k >= 2)

            @pl.when(k >= 1)
            def _():
                va = dot(RT[:, 0:H], T2[was, 0])
                VR[:, 0:H] = va
                VR[:, H:N] = dot(RT[:, H:N] - dot(va, G[was]), T2[was, 1])
                sendR[...] = dot(VR[...], VX[...])

                @pl.when(e_prev)
                def _():
                    r_copy(kp, peer_prev).start()

        def quarter(i, _):
            h = i // 2
            inv = leaf(DW[7 * h + 2 * (i - 2 * h)], scr)

            @pl.when(i == 0)
            def _():
                take(1)

            @pl.when(i == 2 * h)
            def _():
                T2[slot, h, 0:T, 0:T] = inv
                g = dot(DW[7 * h + 1], inv)
                DW[7 * h + 2] = DW[7 * h + 2] - dot(g, g)
                W[...] = dot(g, inv, NN)

            @pl.when(i == 2 * h + 1)
            def _():
                T2[slot, h, T:H, T:H] = inv
                T2[slot, h, T:H, 0:T] = -dot(inv, W[...], NN)

            @pl.when(i == 1)
            def _():
                take(2)
                ba = jnp.concatenate(
                    [
                        jnp.concatenate([DW[3], DW[5]], 1),
                        jnp.concatenate([DW[4], DW[6]], 1),
                    ],
                    0,
                )
                g = dot(ba, T2[slot, 0])
                G[slot] = g
                gg = dot(g, g)
                take(3)
                DW[7] = DW[7] - gg[0:T, 0:T]
                DW[8] = DW[8] - gg[T:H, 0:T]
                DW[9] = DW[9] - gg[T:H, T:H]
                rhs()

            return 0

        lax.fori_loop(0, 4, quarter, 0)

        @pl.when(k < levels)
        def _():
            @pl.when(k == 0)
            def _():
                finish_first()

            def solve(h):
                rows = slice(h * H, h * H + H)

                @pl.when(e_prev)
                def _():
                    p_copy(h, kp, peer_prev).wait_recv()

                @pl.when(k >= 1)
                def _():
                    v_copy(h, kp).wait_send()

                va = dot(recvP[k, rows, 0:H], T2[slot, 0])
                VX[rows, 0:H] = va
                VX[rows, H:N] = dot(recvP[k, rows, H:N] - dot(va, G[slot]), T2[slot, 1])

                @pl.when(k < levels - 1)
                def _():
                    v_copy(h, k).start()

            def diagonal(i, j, pieces):
                qq = dot(VX[i * H : i * H + H, :], VX[j * H : j * H + H, :])
                for p in pieces:

                    @pl.when(e_prev)
                    def _():
                        q_copy(p, kp, peer_prev).wait_send()

                    for n in range(PIECES[p][0], PIECES[p][0] + PIECES[p][1]):
                        r0, c0 = TILES[n][0] * T - i * H, TILES[n][1] * T - j * H
                        sendQ[n] = qq[r0 : r0 + T, c0 : c0 + T]

                    @pl.when(e)
                    def _():
                        q_copy(p, k, peer).start()

            solve(0)
            diagonal(0, 0, (0, 1))
            solve(1)
            diagonal(1, 0, (2,))
            diagonal(1, 1, (3,))

        @pl.when(k < levels - 1)
        def _():
            def product(h, _):
                rows = pl.ds(pl.multiple_of(h * H, H), H)
                v_copy(h, k).wait_recv()

                @pl.when(e_prev)
                def _():
                    p_copy(h, kp, peer_prev).wait_send()

                sendP[rows, :] = dot(VY[k, rows, :], VX[...])

                @pl.when(e)
                def _():
                    p_copy(h, k, peer).start()

                @pl.when(jnp.logical_not(e))
                def _():
                    recvP[k + 1, rows, :] = jnp.zeros((H, N), F32)

                return 0

            lax.fori_loop(0, 2, product, 0)

        @pl.when((k == levels - 1) & e_prev)
        def _():
            p_copy(0, kp, peer_prev).wait_send()
            p_copy(1, kp, peer_prev).wait_send()

        @pl.when(k == levels)
        def _():
            take_rhs(kp, prev, k >= 1)

        @pl.when((k == levels) & e_prev)
        def _():
            for p in range(len(PIECES)):
                q_copy(p, kp, peer_prev).wait_send()

        return d * 2

    lax.fori_loop(0, levels + 1, step, 1)

    end = levels % 2
    va = dot(RT[own_rt, 0:H], T2[end, 0])
    vb = dot(RT[own_rt, H:N] - dot(va, G[end]), T2[end, 1])
    xb = dot(vb, T2[end, 1], NN)
    xa = dot(va - dot(xb, G[end], NN), T2[end, 0], NN)
    out[0:H, :] = xa.T
    out[H:N, :] = xb.T


def solution(mesh):
    slabs = mesh.shape["slab"]
    levels = (slabs - 1).bit_length()

    def on_device(coupling, tile_pattern, orbital_mass, sources):
        column = lax.axis_index("col")
        pattern = tile_pattern[0]
        mask = jnp.broadcast_to(
            pattern.T[:, None, :, None].astype(F32), (N // T // 2, T, N // T, T)
        ).reshape(H, N)
        rows = lax.broadcasted_iota(jnp.int32, (H, N), 0) + column * H
        cols = lax.broadcasted_iota(jnp.int32, (H, N), 1)
        brow = (rows == cols).astype(F32) + mask * coupling[0].T
        both = jnp.concatenate([orbital_mass[0], orbital_mass[0]])
        mine = (jnp.arange(N) // H == column).astype(F32)
        mrow = jnp.broadcast_to((both * mine)[None], (8, N))
        dma = pltpu.SemaphoreType.DMA
        vmem = pl.BlockSpec(memory_space=pltpu.VMEM)
        x = pl.pallas_call(
            functools.partial(kernel, slabs, levels),
            out_shape=jax.ShapeDtypeStruct((N, T), F32),
            in_specs=[vmem] * 3,
            out_specs=vmem,
            scratch_shapes=[
                pltpu.VMEM((levels, N, N), F32),
                pltpu.VMEM((levels, 10, T, T), F32),
                pltpu.VMEM((levels, 10, T, T), F32),
                pltpu.VMEM((levels, M, N), F32),
                pltpu.VMEM((levels, M, N), F32),
                pltpu.VMEM((levels, N, N), F32),
                pltpu.VMEM((N, N), F32),
                pltpu.VMEM((N, N), F32),
                pltpu.VMEM((M, N), F32),
                pltpu.VMEM((M, N), F32),
                pltpu.VMEM((10, T, T), F32),
                pltpu.VMEM((10, T, T), F32),
                pltpu.VMEM((2, 2, H, H), F32),
                pltpu.VMEM((2, H, H), F32),
                pltpu.VMEM((T, T), F32),
                pltpu.VMEM((18, 8, T), F32),
                pltpu.VMEM((8, N), F32),
                pltpu.VMEM((10, T, T), F32),
                pltpu.VMEM((N, N), F32),
                pltpu.VMEM((M, N), F32),
                dma((3,)),
                dma((3,)),
                dma((3,)),
                dma((3,)),
                dma((2,)),
                dma((2,)),
                dma((2,)),
                dma((levels, 2)),
                dma((len(PIECES),)),
                dma((levels, len(PIECES))),
                dma((len(PIECES),)),
                dma((levels, len(PIECES))),
                dma((2,)),
                dma((levels, 2)),
                dma(()),
                dma((levels,)),
                dma(()),
                dma((levels,)),
            ],
            compiler_params=pltpu.CompilerParams(
                collective_id=0, has_side_effects=True, vmem_limit_bytes=56 << 20
            ),
        )(brow, sources[0], mrow)
        return x[None]

    placed = (
        P("slab", None, "col"),
        P("slab", None, "col"),
        P("slab", "col"),
        P("slab", None, "col"),
    )
    return jax.shard_map(
        on_device, mesh=mesh, in_specs=placed, out_specs=P("slab", None, "col"), check_vma=False
    )
```

```python
import functools

import jax
import jax.numpy as jnp
from jax import lax
from jax.experimental import pallas as pl
from jax.experimental.pallas import tpu as pltpu
from jax.sharding import PartitionSpec as P

F32 = jnp.float32
N = 512
H = 256
T = 128
M = 256
NT = (((1,), (1,)), ((), ()))
NN = (((1,), (0,)), ((), ()))
TILES = ((0, 0), (1, 0), (1, 1), (2, 0), (3, 0), (2, 1), (3, 1), (2, 2), (3, 2), (3, 3))
PIECES = ((0, 1), (1, 2), (3, 4), (7, 3))
MESH = pl.DeviceIdType.MESH


def dot(a, b, dims=NT):
    return lax.dot_general(
        a, b, dims, precision=lax.Precision.HIGHEST, preferred_element_type=F32
    )


def leaf(block, scr):
    rows = [block[8 * i : 8 * i + 8, :] for i in range(16)]
    lane = lax.broadcasted_iota(jnp.int32, (8, T), 1)
    sub = lax.broadcasted_iota(jnp.int32, (8, T), 0)
    out = []
    for J in range(16):
        b = (J % 2) * 9
        own = (lane >= 8 * J) & (lane < 8 * J + 8)
        for j in range(8):
            scr[b + j] = jnp.broadcast_to(rows[J][:, 8 * J + j : 8 * J + j + 1], (8, T))
        scr[b + 8] = jnp.where(own, jnp.where(lane == sub + 8 * J, 1.0, 0.0), rows[J])
        R = [jnp.broadcast_to(scr[b + 8, i : i + 1, :], (8, T)) for i in range(8)]
        E = [[None] * 8 for _ in range(8)]
        for i in range(8):
            for j in range(i + 1):
                E[i][j] = E[j][i] = jnp.broadcast_to(scr[b + j, i : i + 1, :], (8, T))
        V = [None] * 8
        for j in range(0, 8, 2):
            a, c, e = E[j][j], E[j][j + 1], E[j + 1][j + 1]
            q = 1.0 / (a * e - c * c)
            r = c * (1.0 / a)
            V[j] = R[j] * lax.rsqrt(a)
            V[j + 1] = (R[j + 1] - r * R[j]) * lax.rsqrt(e - c * r)
            ia, ic, ie = e * q, c * q, a * q
            R[j], R[j + 1] = ia * R[j] - ic * R[j + 1], ie * R[j + 1] - ic * R[j]
            for k in range(j + 2, 8):
                E[j][k], E[j + 1][k] = (
                    ia * E[j][k] - ic * E[j + 1][k],
                    ie * E[j + 1][k] - ic * E[j][k],
                )
            for i in range(8):
                if i in (j, j + 1):
                    continue
                m0, m1 = E[i][j], E[i][j + 1]
                R[i] = R[i] - (m0 * R[j] + m1 * R[j + 1])
                for k in range(j + 2, 8):
                    if i < j or k >= i:
                        E[i][k] = E[i][k] - (m0 * E[j][k] + m1 * E[j + 1][k])
            for i in range(j + 2, 8):
                for k in range(j + 2, i):
                    E[i][k] = E[k][i]
        for i in range(J + 1, 16):
            t = None
            for k in range(8):
                c = jnp.broadcast_to(rows[i][:, 8 * J + k : 8 * J + k + 1], (8, T)) * R[k]
                t = c if t is None else t + c
            rows[i] = jnp.where(own, 0.0, rows[i]) - t
        z = V[0]
        for r in range(1, 8):
            z = jnp.where(sub == r, V[r], z)
        out.append(jnp.where(lane <= sub + 8 * J, z, 0.0))
    return jnp.concatenate(out, 0)


def kernel(
    slabs,
    levels,
    brow,
    src,
    mrow,
    out,
    recvP,
    recvQ,
    sibQ,
    recvR,
    sibR,
    VY,
    O,
    VX,
    VR,
    RT,
    D,
    DW,
    T2,
    G,
    W,
    scr,
    mb,
    sendQ,
    sendP,
    sendR,
    i_send,
    i_recv,
    n_send,
    n_recv,
    f_send,
    f_recv,
    v_send,
    v_recv,
    q_send,
    q_recv,
    qf_send,
    qf_recv,
    p_send,
    p_recv,
    r_send,
    r_recv,
    rf_send,
    rf_recv,
):
    s = lax.axis_index("slab")
    c = lax.axis_index("col")
    sgn = 2 * c - 1
    sib = 1 - c

    def inside(t):
        return (t >= 0) & (t < slabs)

    def remote(src, dst, ss, rs, slab, col):
        return pltpu.make_async_remote_copy(
            src_ref=src,
            dst_ref=dst,
            send_sem=ss,
            recv_sem=rs,
            device_id={"slab": slab, "col": col},
            device_id_type=MESH,
        )

    barrier = pltpu.get_barrier_semaphore()
    pl.semaphore_signal(barrier, inc=1, device_id={"slab": s, "col": sib}, device_id_type=MESH)
    count = 1
    for k in range(levels):
        peer = s + sgn * 2**k
        here = inside(peer)
        count = count + here.astype(jnp.int32)

        @pl.when(here)
        def _():
            pl.semaphore_signal(
                barrier, inc=1, device_id={"slab": peer, "col": sib}, device_id_type=MESH
            )

    pl.semaphore_wait(barrier, count)

    first = recvP.at[0]
    own_rt = pl.ds(pl.multiple_of(c * T, T), T)
    RT[own_rt, :] = src[...].T
    to_sib = functools.partial(remote, slab=s, col=sib)
    cp_m = to_sib(mrow, mb, i_send.at[0], i_recv.at[0])
    cp_r = to_sib(RT.at[own_rt], RT.at[own_rt], i_send.at[1], i_recv.at[1])
    low, high, full = pl.ds(0, H), pl.ds(H, H), pl.ds(0, N)
    cp_b0 = to_sib(brow, first.at[low], i_send.at[2], i_recv.at[2])
    cp_b1 = to_sib(brow, O.at[high], i_send.at[2], i_recv.at[2])
    parts = ((low, low), (high, full), (low, high))
    nxt = [
        remote(first.at[p], first.at[p], n_send.at[i], n_recv.at[i], s + 1, 0)
        for i, p in enumerate(parts)
    ]
    fwd = [to_sib(first.at[p], O.at[p], f_send.at[i], f_recv.at[i]) for i, p in enumerate(parts[:2])]
    has_next, has_prior = s < slabs - 1, s > 0

    @pl.when(c == 0)
    def _():
        cp_b0.start()
        O[0:H, :] = brow[...]

        @pl.when(s == 0)
        def _():
            first[...] = jnp.zeros((N, N), F32)

    @pl.when(c == 1)
    def _():
        cp_b1.start()
        first[H:N, :] = brow[...]
        cp_b0.wait_recv()

        @pl.when(has_next)
        def _():
            for copy in nxt:
                copy.start()

        @pl.when(s == 0)
        def _():
            O[...] = jnp.zeros((N, N), F32)

    cp_m.start()
    cp_r.start()
    cp_m.wait()
    cp_r.wait()

    @pl.when(c == 0)
    def _():
        cp_b1.wait_recv()
        cp_b0.wait_send()

    @pl.when(c == 1)
    def _():
        cp_b1.wait_send()

    def arrive(part):
        @pl.when((c == 0) & has_prior)
        def _():
            nxt[part].wait_recv()
            fwd[part].start()

        @pl.when((c == 1) & has_prior)
        def _():
            fwd[part].wait_recv()

    eye = lax.broadcasted_iota(jnp.int32, (T, T), 0) == lax.broadcasted_iota(jnp.int32, (T, T), 1)

    def build(p):
        for n in range(PIECES[p][0], PIECES[p][0] + PIECES[p][1]):
            i, j = TILES[n]
            rr, cc = slice(T * i, T * i + T), slice(T * j, T * j + T)
            tile = first[rr, cc] + O[rr, cc]
            if i == j:
                mass = mrow[0:1, cc] + mb[0:1, cc]
                tile = tile + jnp.where(eye, jnp.broadcast_to(mass, (T, T)), 0.0)
            D[n] = tile

    def finish_first():
        @pl.when((c == 0) & has_prior)
        def _():
            nxt[2].wait_recv()
            fwd[0].wait_send()
            fwd[1].wait_send()

        @pl.when((c == 1) & has_next)
        def _():
            for copy in nxt:
                copy.wait_send()

        @pl.when((c == 1) & jnp.logical_not(has_next))
        def _():
            first[...] = jnp.zeros((N, N), F32)

    T2[...] = jnp.zeros((2, 2, H, H), F32)

    def step(k, d):
        prev = d // 2
        slot, was = k % 2, (k + 1) % 2
        e = inside(s + sgn * d) & (k < levels)
        e_prev = inside(s + sgn * prev) & (k >= 1)
        e_sib = inside(s - sgn * prev) & (k >= 1)
        kp = jnp.maximum(k - 1, 0)
        peer = s + sgn * d
        peer_prev = s + sgn * prev

        def q_copy(p, level, to):
            o, n = PIECES[p]
            return remote(
                sendQ.at[pl.ds(o, n)],
                recvQ.at[level, pl.ds(o, n)],
                q_send.at[p],
                q_recv.at[level, p],
                to,
                sib,
            )

        def q_forward(p, level):
            o, n = PIECES[p]
            return to_sib(
                recvQ.at[level, pl.ds(o, n)],
                sibQ.at[level, pl.ds(o, n)],
                qf_send.at[p],
                qf_recv.at[level, p],
            )

        def p_copy(h, level, to):
            rows = pl.ds(pl.multiple_of(h * H, H), H)
            return remote(
                sendP.at[rows],
                recvP.at[level + 1, rows],
                p_send.at[h],
                p_recv.at[level, h],
                to,
                sib,
            )

        def v_copy(h, level):
            rows = pl.ds(pl.multiple_of(h * H, H), H)
            return to_sib(VX.at[rows], VY.at[level, rows], v_send.at[h], v_recv.at[level, h])

        def r_copy(level, to):
            return remote(sendR, recvR.at[level], r_send, r_recv.at[level], to, sib)

        def r_forward(level):
            return to_sib(recvR.at[level], sibR.at[level], rf_send, rf_recv.at[level])

        def pass_on(p):
            @pl.when(e_prev)
            def _():
                q_copy(p, kp, peer_prev).wait_recv()
                q_forward(p, kp).start()

        def take(p):
            o, n = PIECES[p]

            @pl.when(k == 0)
            def _():
                if p in (0, 2):
                    arrive(p // 2)
                build(p)

            @pl.when(e_prev)
            def _():
                D[o : o + n] = D[o : o + n] - recvQ[kp, o : o + n]

            @pl.when(e_sib)
            def _():
                q_forward(p, kp).wait_recv()
                D[o : o + n] = D[o : o + n] - sibQ[kp, o : o + n]

            DW[o : o + n] = D[o : o + n]

            @pl.when(e_prev)
            def _():
                q_forward(p, kp).wait_send()

        pass_on(0)
        pass_on(1)
        take(0)

        def pass_on_rhs(level, stride, on):
            there = s + sgn * stride

            @pl.when(on & inside(there))
            def _():
                r_copy(level, there).wait_recv()
                r_forward(level).start()

        def take_rhs(level, stride, on):
            there = s + sgn * stride

            @pl.when(on & inside(there))
            def _():
                RT[...] = RT[...] + recvR[level]

            @pl.when(on & inside(s - sgn * stride))
            def _():
                r_forward(level).wait_recv()
                RT[...] = RT[...] + sibR[level]

            @pl.when(on & inside(there))
            def _():
                r_forward(level).wait_send()
                r_copy(level, there).wait_send()

        def rhs():
            take_rhs(jnp.maximum(k - 2, 0), d // 4, k >= 2)

            @pl.when(k >= 1)
            def _():
                va = dot(RT[:, 0:H], T2[was, 0])
                VR[:, 0:H] = va
                VR[:, H:N] = dot(RT[:, H:N] - dot(va, G[was]), T2[was, 1])
                sendR[...] = dot(VR[...], VX[...])

                @pl.when(e_prev)
                def _():
                    r_copy(kp, peer_prev).start()

        def quarter(i, _):
            h = i // 2
            inv = leaf(DW[7 * h + 2 * (i - 2 * h)], scr)

            @pl.when(i == 0)
            def _():
                take(1)

            @pl.when(i == 2 * h)
            def _():
                T2[slot, h, 0:T, 0:T] = inv
                g = dot(DW[7 * h + 1], inv)
                DW[7 * h + 2] = DW[7 * h + 2] - dot(g, g)
                W[...] = dot(g, inv, NN)

                @pl.when(i == 0)
                def _():
                    pass_on(2)

            @pl.when(i == 2 * h + 1)
            def _():
                T2[slot, h, T:H, T:H] = inv
                T2[slot, h, T:H, 0:T] = -dot(inv, W[...], NN)

            @pl.when(i == 1)
            def _():
                pass_on(3)
                pass_on_rhs(jnp.maximum(k - 2, 0), d // 4, k >= 2)
                take(2)
                ba = jnp.concatenate(
                    [
                        jnp.concatenate([DW[3], DW[5]], 1),
                        jnp.concatenate([DW[4], DW[6]], 1),
                    ],
                    0,
                )
                g = dot(ba, T2[slot, 0])
                G[slot] = g
                gg = dot(g, g)
                take(3)
                DW[7] = DW[7] - gg[0:T, 0:T]
                DW[8] = DW[8] - gg[T:H, 0:T]
                DW[9] = DW[9] - gg[T:H, T:H]
                rhs()

            return 0

        lax.fori_loop(0, 4, quarter, 0)

        @pl.when(k < levels)
        def _():
            @pl.when(k == 0)
            def _():
                finish_first()

            def solve(h):
                rows = slice(h * H, h * H + H)

                @pl.when(e_prev)
                def _():
                    p_copy(h, kp, peer_prev).wait_recv()

                @pl.when(k >= 1)
                def _():
                    v_copy(h, kp).wait_send()

                va = dot(recvP[k, rows, 0:H], T2[slot, 0])
                VX[rows, 0:H] = va
                VX[rows, H:N] = dot(recvP[k, rows, H:N] - dot(va, G[slot]), T2[slot, 1])

                @pl.when(k < levels - 1)
                def _():
                    v_copy(h, k).start()

            def diagonal(i, j, pieces):
                qq = dot(VX[i * H : i * H + H, :], VX[j * H : j * H + H, :])
                for p in pieces:

                    @pl.when(e_prev)
                    def _():
                        q_copy(p, kp, peer_prev).wait_send()

                    for n in range(PIECES[p][0], PIECES[p][0] + PIECES[p][1]):
                        r0, c0 = TILES[n][0] * T - i * H, TILES[n][1] * T - j * H
                        sendQ[n] = qq[r0 : r0 + T, c0 : c0 + T]

                    @pl.when(e)
                    def _():
                        q_copy(p, k, peer).start()

            solve(0)
            diagonal(0, 0, (0, 1))
            solve(1)
            diagonal(1, 0, (2,))
            diagonal(1, 1, (3,))

        @pl.when(k < levels - 1)
        def _():
            def product(h, _):
                rows = pl.ds(pl.multiple_of(h * H, H), H)
                v_copy(h, k).wait_recv()

                @pl.when(e_prev)
                def _():
                    p_copy(h, kp, peer_prev).wait_send()

                sendP[rows, :] = dot(VY[k, rows, :], VX[...])

                @pl.when(e)
                def _():
                    p_copy(h, k, peer).start()

                @pl.when(jnp.logical_not(e))
                def _():
                    recvP[k + 1, rows, :] = jnp.zeros((H, N), F32)

                return 0

            lax.fori_loop(0, 2, product, 0)

        @pl.when((k == levels - 1) & e_prev)
        def _():
            p_copy(0, kp, peer_prev).wait_send()
            p_copy(1, kp, peer_prev).wait_send()

        @pl.when(k == levels)
        def _():
            pass_on_rhs(kp, prev, k >= 1)
            take_rhs(kp, prev, k >= 1)

        @pl.when((k == levels) & e_prev)
        def _():
            for p in range(len(PIECES)):
                q_copy(p, kp, peer_prev).wait_send()

        return d * 2

    lax.fori_loop(0, levels + 1, step, 1)

    end = levels % 2
    va = dot(RT[own_rt, 0:H], T2[end, 0])
    vb = dot(RT[own_rt, H:N] - dot(va, G[end]), T2[end, 1])
    xb = dot(vb, T2[end, 1], NN)
    xa = dot(va - dot(xb, G[end], NN), T2[end, 0], NN)
    out[0:H, :] = xa.T
    out[H:N, :] = xb.T


def solution(mesh):
    slabs = mesh.shape["slab"]
    levels = (slabs - 1).bit_length()

    def on_device(coupling, tile_pattern, orbital_mass, sources):
        column = lax.axis_index("col")
        pattern = tile_pattern[0]
        mask = jnp.broadcast_to(
            pattern.T[:, None, :, None].astype(F32), (N // T // 2, T, N // T, T)
        ).reshape(H, N)
        rows = lax.broadcasted_iota(jnp.int32, (H, N), 0) + column * H
        cols = lax.broadcasted_iota(jnp.int32, (H, N), 1)
        brow = (rows == cols).astype(F32) + mask * coupling[0].T
        both = jnp.concatenate([orbital_mass[0], orbital_mass[0]])
        mine = (jnp.arange(N) // H == column).astype(F32)
        mrow = jnp.broadcast_to((both * mine)[None], (8, N))
        dma = pltpu.SemaphoreType.DMA
        vmem = pl.BlockSpec(memory_space=pltpu.VMEM)
        x = pl.pallas_call(
            functools.partial(kernel, slabs, levels),
            out_shape=jax.ShapeDtypeStruct((N, T), F32),
            in_specs=[vmem] * 3,
            out_specs=vmem,
            scratch_shapes=[
                pltpu.VMEM((levels, N, N), F32),
                pltpu.VMEM((levels, 10, T, T), F32),
                pltpu.VMEM((levels, 10, T, T), F32),
                pltpu.VMEM((levels, M, N), F32),
                pltpu.VMEM((levels, M, N), F32),
                pltpu.VMEM((levels, N, N), F32),
                pltpu.VMEM((N, N), F32),
                pltpu.VMEM((N, N), F32),
                pltpu.VMEM((M, N), F32),
                pltpu.VMEM((M, N), F32),
                pltpu.VMEM((10, T, T), F32),
                pltpu.VMEM((10, T, T), F32),
                pltpu.VMEM((2, 2, H, H), F32),
                pltpu.VMEM((2, H, H), F32),
                pltpu.VMEM((T, T), F32),
                pltpu.VMEM((18, 8, T), F32),
                pltpu.VMEM((8, N), F32),
                pltpu.VMEM((10, T, T), F32),
                pltpu.VMEM((N, N), F32),
                pltpu.VMEM((M, N), F32),
                dma((3,)),
                dma((3,)),
                dma((3,)),
                dma((3,)),
                dma((2,)),
                dma((2,)),
                dma((2,)),
                dma((levels, 2)),
                dma((len(PIECES),)),
                dma((levels, len(PIECES))),
                dma((len(PIECES),)),
                dma((levels, len(PIECES))),
                dma((2,)),
                dma((levels, 2)),
                dma(()),
                dma((levels,)),
                dma(()),
                dma((levels,)),
            ],
            compiler_params=pltpu.CompilerParams(
                collective_id=0, has_side_effects=True, vmem_limit_bytes=56 << 20
            ),
        )(brow, sources[0], mrow)
        return x[None]

    placed = (
        P("slab", None, "col"),
        P("slab", None, "col"),
        P("slab", "col"),
        P("slab", None, "col"),
    )
    return jax.shard_map(
        on_device, mesh=mesh, in_specs=placed, out_specs=P("slab", None, "col"), check_vma=False
    )
```

```python
import functools

import jax
import jax.numpy as jnp
from jax import lax
from jax.experimental import pallas as pl
from jax.experimental.pallas import tpu as pltpu
from jax.sharding import PartitionSpec as P

F32 = jnp.float32
N = 512
H = 256
T = 128
M = 256
NT = (((1,), (1,)), ((), ()))
NN = (((1,), (0,)), ((), ()))
TILES = ((0, 0), (1, 0), (1, 1), (2, 0), (3, 0), (2, 1), (3, 1), (2, 2), (3, 2), (3, 3))
PIECES = ((0, 1), (1, 2), (3, 4), (7, 3))
MESH = pl.DeviceIdType.MESH


def dot(a, b, dims=NT):
    return lax.dot_general(
        a, b, dims, precision=lax.Precision.HIGHEST, preferred_element_type=F32
    )


def leaf(block, scr):
    rows = [block[8 * i : 8 * i + 8, :] for i in range(16)]
    lane = lax.broadcasted_iota(jnp.int32, (8, T), 1)
    sub = lax.broadcasted_iota(jnp.int32, (8, T), 0)
    out = []
    for J in range(16):
        b = (J % 2) * 9
        own = (lane >= 8 * J) & (lane < 8 * J + 8)
        for j in range(8):
            scr[b + j] = jnp.broadcast_to(rows[J][:, 8 * J + j : 8 * J + j + 1], (8, T))
        scr[b + 8] = jnp.where(own, jnp.where(lane == sub + 8 * J, 1.0, 0.0), rows[J])
        R = [jnp.broadcast_to(scr[b + 8, i : i + 1, :], (8, T)) for i in range(8)]
        E = [[None] * 8 for _ in range(8)]
        for i in range(8):
            for j in range(i + 1):
                E[i][j] = E[j][i] = jnp.broadcast_to(scr[b + j, i : i + 1, :], (8, T))
        V = [None] * 8
        for j in range(0, 8, 2):
            a, c, e = E[j][j], E[j][j + 1], E[j + 1][j + 1]
            q = 1.0 / (a * e - c * c)
            r = c * (1.0 / a)
            V[j] = R[j] * lax.rsqrt(a)
            V[j + 1] = (R[j + 1] - r * R[j]) * lax.rsqrt(e - c * r)
            ia, ic, ie = e * q, c * q, a * q
            R[j], R[j + 1] = ia * R[j] - ic * R[j + 1], ie * R[j + 1] - ic * R[j]
            for k in range(j + 2, 8):
                E[j][k], E[j + 1][k] = (
                    ia * E[j][k] - ic * E[j + 1][k],
                    ie * E[j + 1][k] - ic * E[j][k],
                )
            for i in range(8):
                if i in (j, j + 1):
                    continue
                m0, m1 = E[i][j], E[i][j + 1]
                R[i] = R[i] - (m0 * R[j] + m1 * R[j + 1])
                for k in range(j + 2, 8):
                    if i < j or k >= i:
                        E[i][k] = E[i][k] - (m0 * E[j][k] + m1 * E[j + 1][k])
            for i in range(j + 2, 8):
                for k in range(j + 2, i):
                    E[i][k] = E[k][i]
        for i in range(J + 1, 16):
            t = None
            for k in range(8):
                c = jnp.broadcast_to(rows[i][:, 8 * J + k : 8 * J + k + 1], (8, T)) * R[k]
                t = c if t is None else t + c
            rows[i] = jnp.where(own, 0.0, rows[i]) - t
        z = V[0]
        for r in range(1, 8):
            z = jnp.where(sub == r, V[r], z)
        out.append(jnp.where(lane <= sub + 8 * J, z, 0.0))
    return jnp.concatenate(out, 0)


def kernel(
    slabs,
    levels,
    brow,
    src,
    mrow,
    out,
    recvP,
    recvQ,
    sibQ,
    recvR,
    sibR,
    VY,
    O,
    VX,
    VR,
    RT,
    D,
    DW,
    T2,
    G,
    W,
    scr,
    mb,
    sendQ,
    sendP,
    sendR,
    i_send,
    i_recv,
    n_send,
    n_recv,
    f_send,
    f_recv,
    v_send,
    v_recv,
    q_send,
    q_recv,
    qf_send,
    qf_recv,
    p_send,
    p_recv,
    r_send,
    r_recv,
    rf_send,
    rf_recv,
):
    s = lax.axis_index("slab")
    c = lax.axis_index("col")
    sgn = 2 * c - 1
    sib = 1 - c

    def inside(t):
        return (t >= 0) & (t < slabs)

    def remote(src, dst, ss, rs, slab, col):
        return pltpu.make_async_remote_copy(
            src_ref=src,
            dst_ref=dst,
            send_sem=ss,
            recv_sem=rs,
            device_id={"slab": slab, "col": col},
            device_id_type=MESH,
        )

    barrier = pltpu.get_barrier_semaphore()
    pl.semaphore_signal(barrier, inc=1, device_id={"slab": s, "col": sib}, device_id_type=MESH)
    count = 1
    for k in range(levels):
        peer = s + sgn * 2**k
        here = inside(peer)
        count = count + here.astype(jnp.int32)

        @pl.when(here)
        def _():
            pl.semaphore_signal(
                barrier, inc=1, device_id={"slab": peer, "col": sib}, device_id_type=MESH
            )

    pl.semaphore_wait(barrier, count)

    first = recvP.at[0]
    own_rt = pl.ds(pl.multiple_of(c * T, T), T)
    RT[own_rt, :] = src[...].T
    to_sib = functools.partial(remote, slab=s, col=sib)
    cp_m = to_sib(mrow, mb, i_send.at[0], i_recv.at[0])
    cp_r = to_sib(RT.at[own_rt], RT.at[own_rt], i_send.at[1], i_recv.at[1])
    low, high, full = pl.ds(0, H), pl.ds(H, H), pl.ds(0, N)
    cp_b0 = to_sib(brow, first.at[low], i_send.at[2], i_recv.at[2])
    cp_b1 = to_sib(brow, O.at[high], i_send.at[2], i_recv.at[2])
    parts = ((low, low), (high, full), (low, high))
    nxt = [
        remote(first.at[p], first.at[p], n_send.at[i], n_recv.at[i], s + 1, 0)
        for i, p in enumerate(parts)
    ]
    fwd = [to_sib(first.at[p], O.at[p], f_send.at[i], f_recv.at[i]) for i, p in enumerate(parts[:2])]
    has_next, has_prior = s < slabs - 1, s > 0

    @pl.when(c == 0)
    def _():
        cp_b0.start()
        O[0:H, :] = brow[...]

        @pl.when(s == 0)
        def _():
            first[...] = jnp.zeros((N, N), F32)

    @pl.when(c == 1)
    def _():
        cp_b1.start()
        first[H:N, :] = brow[...]
        cp_b0.wait_recv()

        @pl.when(has_next)
        def _():
            for copy in nxt:
                copy.start()

        @pl.when(s == 0)
        def _():
            O[...] = jnp.zeros((N, N), F32)

    cp_m.start()
    cp_r.start()
    cp_m.wait()
    cp_r.wait()

    @pl.when(c == 0)
    def _():
        cp_b1.wait_recv()
        cp_b0.wait_send()

    @pl.when(c == 1)
    def _():
        cp_b1.wait_send()

    def arrive(part):
        @pl.when((c == 0) & has_prior)
        def _():
            nxt[part].wait_recv()
            fwd[part].start()

        @pl.when((c == 1) & has_prior)
        def _():
            fwd[part].wait_recv()

    eye = lax.broadcasted_iota(jnp.int32, (T, T), 0) == lax.broadcasted_iota(jnp.int32, (T, T), 1)

    def build(p):
        for n in range(PIECES[p][0], PIECES[p][0] + PIECES[p][1]):
            i, j = TILES[n]
            rr, cc = slice(T * i, T * i + T), slice(T * j, T * j + T)
            tile = first[rr, cc] + O[rr, cc]
            if i == j:
                mass = mrow[0:1, cc] + mb[0:1, cc]
                tile = tile + jnp.where(eye, jnp.broadcast_to(mass, (T, T)), 0.0)
            D[n] = tile

    def finish_first():
        @pl.when((c == 0) & has_prior)
        def _():
            nxt[2].wait_recv()
            fwd[0].wait_send()
            fwd[1].wait_send()

        @pl.when((c == 1) & has_next)
        def _():
            for copy in nxt:
                copy.wait_send()

        @pl.when((c == 1) & jnp.logical_not(has_next))
        def _():
            first[...] = jnp.zeros((N, N), F32)

    T2[...] = jnp.zeros((2, 2, H, H), F32)

    def step(k, d):
        prev = d // 2
        slot, was = k % 2, (k + 1) % 2
        e = inside(s + sgn * d) & (k < levels)
        e_prev = inside(s + sgn * prev) & (k >= 1)
        e_sib = inside(s - sgn * prev) & (k >= 1)
        kp = jnp.maximum(k - 1, 0)
        peer = s + sgn * d
        peer_prev = s + sgn * prev

        def q_copy(p, level, to):
            o, n = PIECES[p]
            return remote(
                sendQ.at[pl.ds(o, n)],
                recvQ.at[level, pl.ds(o, n)],
                q_send.at[p],
                q_recv.at[level, p],
                to,
                sib,
            )

        def q_forward(p, level):
            o, n = PIECES[p]
            return to_sib(
                recvQ.at[level, pl.ds(o, n)],
                sibQ.at[level, pl.ds(o, n)],
                qf_send.at[p],
                qf_recv.at[level, p],
            )

        def p_copy(h, level, to):
            rows = pl.ds(pl.multiple_of(h * H, H), H)
            return remote(
                sendP.at[rows],
                recvP.at[level + 1, rows],
                p_send.at[h],
                p_recv.at[level, h],
                to,
                sib,
            )

        def v_copy(h, level):
            rows = pl.ds(pl.multiple_of(h * H, H), H)
            return to_sib(VX.at[rows], VY.at[level, rows], v_send.at[h], v_recv.at[level, h])

        def r_copy(level, to):
            return remote(sendR, recvR.at[level], r_send, r_recv.at[level], to, sib)

        def r_forward(level):
            return to_sib(recvR.at[level], sibR.at[level], rf_send, rf_recv.at[level])

        def pass_on(p):
            @pl.when(e_prev)
            def _():
                q_copy(p, kp, peer_prev).wait_recv()
                q_forward(p, kp).start()

        def take(p):
            o, n = PIECES[p]

            @pl.when(k == 0)
            def _():
                if p in (0, 2):
                    arrive(p // 2)
                build(p)

            @pl.when(e_prev)
            def _():
                D[o : o + n] = D[o : o + n] - recvQ[kp, o : o + n]

            @pl.when(e_sib)
            def _():
                q_forward(p, kp).wait_recv()
                D[o : o + n] = D[o : o + n] - sibQ[kp, o : o + n]

            DW[o : o + n] = D[o : o + n]

            @pl.when(e_prev)
            def _():
                q_forward(p, kp).wait_send()

        pass_on(0)
        pass_on(1)
        take(0)

        def pass_on_rhs(level, stride, on):
            there = s + sgn * stride

            @pl.when(on & inside(there))
            def _():
                r_copy(level, there).wait_recv()
                r_forward(level).start()

        def take_rhs(level, stride, on):
            there = s + sgn * stride

            @pl.when(on & inside(there))
            def _():
                RT[...] = RT[...] + recvR[level]

            @pl.when(on & inside(s - sgn * stride))
            def _():
                r_forward(level).wait_recv()
                RT[...] = RT[...] + sibR[level]

            @pl.when(on & inside(there))
            def _():
                r_forward(level).wait_send()
                r_copy(level, there).wait_send()

        def start_p(h):
            @pl.when(e_prev & (k < levels))
            def _():
                p_copy(h, kp, peer_prev).start()

        def start_rhs():
            @pl.when(e_prev)
            def _():
                r_copy(kp, peer_prev).start()

        def rhs():
            take_rhs(jnp.maximum(k - 2, 0), d // 4, k >= 2)

            @pl.when(k >= 1)
            def _():
                va = dot(RT[:, 0:H], T2[was, 0])
                VR[:, 0:H] = va
                VR[:, H:N] = dot(RT[:, H:N] - dot(va, G[was]), T2[was, 1])
                sendR[...] = dot(VR[...], VX[...])

                @pl.when(k == levels)
                def _():
                    start_rhs()

        def quarter(i, _):
            h = i // 2
            inv = leaf(DW[7 * h + 2 * (i - 2 * h)], scr)

            @pl.when(i == 0)
            def _():
                take(1)

            @pl.when(i == 2 * h)
            def _():
                T2[slot, h, 0:T, 0:T] = inv
                g = dot(DW[7 * h + 1], inv)
                DW[7 * h + 2] = DW[7 * h + 2] - dot(g, g)
                W[...] = dot(g, inv, NN)

                @pl.when(i == 0)
                def _():
                    pass_on(2)
                    start_p(0)

                @pl.when((i == 2) & (k < levels))
                def _():
                    start_rhs()

            @pl.when(i == 2 * h + 1)
            def _():
                T2[slot, h, T:H, T:H] = inv
                T2[slot, h, T:H, 0:T] = -dot(inv, W[...], NN)

            @pl.when(i == 1)
            def _():
                pass_on(3)
                start_p(1)
                pass_on_rhs(jnp.maximum(k - 2, 0), d // 4, k >= 2)
                take(2)
                ba = jnp.concatenate(
                    [
                        jnp.concatenate([DW[3], DW[5]], 1),
                        jnp.concatenate([DW[4], DW[6]], 1),
                    ],
                    0,
                )
                g = dot(ba, T2[slot, 0])
                G[slot] = g
                gg = dot(g, g)
                take(3)
                DW[7] = DW[7] - gg[0:T, 0:T]
                DW[8] = DW[8] - gg[T:H, 0:T]
                DW[9] = DW[9] - gg[T:H, T:H]
                rhs()

            return 0

        lax.fori_loop(0, 4, quarter, 0)

        @pl.when(k < levels)
        def _():
            @pl.when(k == 0)
            def _():
                finish_first()

            def solve(h):
                rows = slice(h * H, h * H + H)

                @pl.when(e_prev)
                def _():
                    p_copy(h, kp, peer_prev).wait_recv()

                @pl.when(k >= 1)
                def _():
                    v_copy(h, kp).wait_send()

                va = dot(recvP[k, rows, 0:H], T2[slot, 0])
                VX[rows, 0:H] = va
                VX[rows, H:N] = dot(recvP[k, rows, H:N] - dot(va, G[slot]), T2[slot, 1])

                @pl.when(k < levels - 1)
                def _():
                    v_copy(h, k).start()

            def diagonal(i, j, pieces):
                qq = dot(VX[i * H : i * H + H, :], VX[j * H : j * H + H, :])
                for p in pieces:

                    @pl.when(e_prev)
                    def _():
                        q_copy(p, kp, peer_prev).wait_send()

                    for n in range(PIECES[p][0], PIECES[p][0] + PIECES[p][1]):
                        r0, c0 = TILES[n][0] * T - i * H, TILES[n][1] * T - j * H
                        sendQ[n] = qq[r0 : r0 + T, c0 : c0 + T]

                    @pl.when(e)
                    def _():
                        q_copy(p, k, peer).start()

            solve(0)
            diagonal(0, 0, (0, 1))
            solve(1)
            diagonal(1, 0, (2,))
            diagonal(1, 1, (3,))

        @pl.when(k < levels - 1)
        def _():
            def product(h, _):
                rows = pl.ds(pl.multiple_of(h * H, H), H)
                v_copy(h, k).wait_recv()

                @pl.when(e_prev)
                def _():
                    p_copy(h, kp, peer_prev).wait_send()

                sendP[rows, :] = dot(VY[k, rows, :], VX[...])

                @pl.when(jnp.logical_not(e))
                def _():
                    recvP[k + 1, rows, :] = jnp.zeros((H, N), F32)

                return 0

            lax.fori_loop(0, 2, product, 0)

        @pl.when((k == levels - 1) & e_prev)
        def _():
            p_copy(0, kp, peer_prev).wait_send()
            p_copy(1, kp, peer_prev).wait_send()

        @pl.when(k == levels)
        def _():
            pass_on_rhs(kp, prev, k >= 1)
            take_rhs(kp, prev, k >= 1)

        @pl.when((k == levels) & e_prev)
        def _():
            for p in range(len(PIECES)):
                q_copy(p, kp, peer_prev).wait_send()

        return d * 2

    lax.fori_loop(0, levels + 1, step, 1)

    end = levels % 2
    va = dot(RT[own_rt, 0:H], T2[end, 0])
    vb = dot(RT[own_rt, H:N] - dot(va, G[end]), T2[end, 1])
    xb = dot(vb, T2[end, 1], NN)
    xa = dot(va - dot(xb, G[end], NN), T2[end, 0], NN)
    out[0:H, :] = xa.T
    out[H:N, :] = xb.T


def solution(mesh):
    slabs = mesh.shape["slab"]
    levels = (slabs - 1).bit_length()

    def on_device(coupling, tile_pattern, orbital_mass, sources):
        column = lax.axis_index("col")
        pattern = tile_pattern[0]
        mask = jnp.broadcast_to(
            pattern.T[:, None, :, None].astype(F32), (N // T // 2, T, N // T, T)
        ).reshape(H, N)
        rows = lax.broadcasted_iota(jnp.int32, (H, N), 0) + column * H
        cols = lax.broadcasted_iota(jnp.int32, (H, N), 1)
        brow = (rows == cols).astype(F32) + mask * coupling[0].T
        both = jnp.concatenate([orbital_mass[0], orbital_mass[0]])
        mine = (jnp.arange(N) // H == column).astype(F32)
        mrow = jnp.broadcast_to((both * mine)[None], (8, N))
        dma = pltpu.SemaphoreType.DMA
        vmem = pl.BlockSpec(memory_space=pltpu.VMEM)
        x = pl.pallas_call(
            functools.partial(kernel, slabs, levels),
            out_shape=jax.ShapeDtypeStruct((N, T), F32),
            in_specs=[vmem] * 3,
            out_specs=vmem,
            scratch_shapes=[
                pltpu.VMEM((levels, N, N), F32),
                pltpu.VMEM((levels, 10, T, T), F32),
                pltpu.VMEM((levels, 10, T, T), F32),
                pltpu.VMEM((levels, M, N), F32),
                pltpu.VMEM((levels, M, N), F32),
                pltpu.VMEM((levels, N, N), F32),
                pltpu.VMEM((N, N), F32),
                pltpu.VMEM((N, N), F32),
                pltpu.VMEM((M, N), F32),
                pltpu.VMEM((M, N), F32),
                pltpu.VMEM((10, T, T), F32),
                pltpu.VMEM((10, T, T), F32),
                pltpu.VMEM((2, 2, H, H), F32),
                pltpu.VMEM((2, H, H), F32),
                pltpu.VMEM((T, T), F32),
                pltpu.VMEM((18, 8, T), F32),
                pltpu.VMEM((8, N), F32),
                pltpu.VMEM((10, T, T), F32),
                pltpu.VMEM((N, N), F32),
                pltpu.VMEM((M, N), F32),
                dma((3,)),
                dma((3,)),
                dma((3,)),
                dma((3,)),
                dma((2,)),
                dma((2,)),
                dma((2,)),
                dma((levels, 2)),
                dma((len(PIECES),)),
                dma((levels, len(PIECES))),
                dma((len(PIECES),)),
                dma((levels, len(PIECES))),
                dma((2,)),
                dma((levels, 2)),
                dma(()),
                dma((levels,)),
                dma(()),
                dma((levels,)),
            ],
            compiler_params=pltpu.CompilerParams(
                collective_id=0, has_side_effects=True, vmem_limit_bytes=56 << 20
            ),
        )(brow, sources[0], mrow)
        return x[None]

    placed = (
        P("slab", None, "col"),
        P("slab", None, "col"),
        P("slab", "col"),
        P("slab", None, "col"),
    )
    return jax.shard_map(
        on_device, mesh=mesh, in_specs=placed, out_specs=P("slab", None, "col"), check_vma=False
    )
```

```python
import functools

import jax
import jax.numpy as jnp
from jax import lax
from jax.experimental import pallas as pl
from jax.experimental.pallas import tpu as pltpu
from jax.sharding import PartitionSpec as P

F32 = jnp.float32
N = 512
H = 256
T = 128
M = 256
NT = (((1,), (1,)), ((), ()))
NN = (((1,), (0,)), ((), ()))
TILES = ((0, 0), (1, 0), (1, 1), (2, 0), (3, 0), (2, 1), (3, 1), (2, 2), (3, 2), (3, 3))
PIECES = ((0, 1), (1, 2), (3, 4), (7, 3))
MESH = pl.DeviceIdType.MESH


def dot(a, b, dims=NT):
    return lax.dot_general(
        a, b, dims, precision=lax.Precision.HIGHEST, preferred_element_type=F32
    )


def leaf(block, scr):
    rows = [block[8 * i : 8 * i + 8, :] for i in range(16)]
    lane = lax.broadcasted_iota(jnp.int32, (8, T), 1)
    sub = lax.broadcasted_iota(jnp.int32, (8, T), 0)
    out = []
    for J in range(16):
        b = (J % 2) * 9
        own = (lane >= 8 * J) & (lane < 8 * J + 8)
        for j in range(8):
            scr[b + j] = jnp.broadcast_to(rows[J][:, 8 * J + j : 8 * J + j + 1], (8, T))
        scr[b + 8] = jnp.where(own, jnp.where(lane == sub + 8 * J, 1.0, 0.0), rows[J])
        R = [jnp.broadcast_to(scr[b + 8, i : i + 1, :], (8, T)) for i in range(8)]
        E = [[None] * 8 for _ in range(8)]
        for i in range(8):
            for j in range(i + 1):
                E[i][j] = E[j][i] = jnp.broadcast_to(scr[b + j, i : i + 1, :], (8, T))
        V = [None] * 8
        for j in range(0, 8, 2):
            a, c, e = E[j][j], E[j][j + 1], E[j + 1][j + 1]
            q = 1.0 / (a * e - c * c)
            r = c * (1.0 / a)
            V[j] = R[j] * lax.rsqrt(a)
            V[j + 1] = (R[j + 1] - r * R[j]) * lax.rsqrt(e - c * r)
            ia, ic, ie = e * q, c * q, a * q
            R[j], R[j + 1] = ia * R[j] - ic * R[j + 1], ie * R[j + 1] - ic * R[j]
            for k in range(j + 2, 8):
                E[j][k], E[j + 1][k] = (
                    ia * E[j][k] - ic * E[j + 1][k],
                    ie * E[j + 1][k] - ic * E[j][k],
                )
            for i in range(8):
                if i in (j, j + 1):
                    continue
                m0, m1 = E[i][j], E[i][j + 1]
                R[i] = R[i] - (m0 * R[j] + m1 * R[j + 1])
                for k in range(j + 2, 8):
                    if i < j or k >= i:
                        E[i][k] = E[i][k] - (m0 * E[j][k] + m1 * E[j + 1][k])
            for i in range(j + 2, 8):
                for k in range(j + 2, i):
                    E[i][k] = E[k][i]
        for i in range(J + 1, 16):
            t = None
            for k in range(8):
                c = jnp.broadcast_to(rows[i][:, 8 * J + k : 8 * J + k + 1], (8, T)) * R[k]
                t = c if t is None else t + c
            rows[i] = jnp.where(own, 0.0, rows[i]) - t
        z = V[0]
        for r in range(1, 8):
            z = jnp.where(sub == r, V[r], z)
        out.append(jnp.where(lane <= sub + 8 * J, z, 0.0))
    return jnp.concatenate(out, 0)


def kernel(
    slabs,
    levels,
    brow,
    src,
    mrow,
    out,
    recvP,
    recvQ,
    sibQ,
    recvR,
    sibR,
    VY,
    O,
    VX,
    VR,
    RT,
    D,
    DW,
    T2,
    G,
    W,
    scr,
    mb,
    sendQ,
    sendP,
    sendR,
    i_send,
    i_recv,
    n_send,
    n_recv,
    f_send,
    f_recv,
    v_send,
    v_recv,
    q_send,
    q_recv,
    qf_send,
    qf_recv,
    p_send,
    p_recv,
    r_send,
    r_recv,
    rf_send,
    rf_recv,
):
    s = lax.axis_index("slab")
    c = lax.axis_index("col")
    sgn = 2 * c - 1
    sib = 1 - c

    def inside(t):
        return (t >= 0) & (t < slabs)

    def remote(src, dst, ss, rs, slab, col):
        return pltpu.make_async_remote_copy(
            src_ref=src,
            dst_ref=dst,
            send_sem=ss,
            recv_sem=rs,
            device_id={"slab": slab, "col": col},
            device_id_type=MESH,
        )

    barrier = pltpu.get_barrier_semaphore()
    pl.semaphore_signal(barrier, inc=1, device_id={"slab": s, "col": sib}, device_id_type=MESH)
    count = 1
    for k in range(levels):
        peer = s + sgn * 2**k
        here = inside(peer)
        count = count + here.astype(jnp.int32)

        @pl.when(here)
        def _():
            pl.semaphore_signal(
                barrier, inc=1, device_id={"slab": peer, "col": sib}, device_id_type=MESH
            )

    pl.semaphore_wait(barrier, count)

    first = recvP.at[0]
    own_rt = pl.ds(pl.multiple_of(c * T, T), T)
    RT[own_rt, :] = src[...].T
    to_sib = functools.partial(remote, slab=s, col=sib)
    cp_m = to_sib(mrow, mb, i_send.at[0], i_recv.at[0])
    cp_r = to_sib(RT.at[own_rt], RT.at[own_rt], i_send.at[1], i_recv.at[1])
    low, high, full = pl.ds(0, H), pl.ds(H, H), pl.ds(0, N)
    cp_b0 = to_sib(brow, first.at[low], i_send.at[2], i_recv.at[2])
    cp_b1 = to_sib(brow, O.at[high], i_send.at[2], i_recv.at[2])
    parts = ((low, low), (high, full), (low, high))
    nxt = [
        remote(first.at[p], first.at[p], n_send.at[i], n_recv.at[i], s + 1, 0)
        for i, p in enumerate(parts)
    ]
    fwd = [to_sib(first.at[p], O.at[p], f_send.at[i], f_recv.at[i]) for i, p in enumerate(parts[:2])]
    has_next, has_prior = s < slabs - 1, s > 0

    @pl.when(c == 0)
    def _():
        cp_b0.start()
        O[0:H, :] = brow[...]

        @pl.when(s == 0)
        def _():
            first[...] = jnp.zeros((N, N), F32)

    @pl.when(c == 1)
    def _():
        cp_b1.start()
        first[H:N, :] = brow[...]
        cp_b0.wait_recv()

        @pl.when(has_next)
        def _():
            for copy in nxt:
                copy.start()

        @pl.when(s == 0)
        def _():
            O[...] = jnp.zeros((N, N), F32)

    cp_m.start()
    cp_r.start()
    cp_m.wait()
    cp_r.wait()

    @pl.when(c == 0)
    def _():
        cp_b1.wait_recv()
        cp_b0.wait_send()

    @pl.when(c == 1)
    def _():
        cp_b1.wait_send()

    def arrive(part):
        @pl.when((c == 0) & has_prior)
        def _():
            nxt[part].wait_recv()
            fwd[part].start()

        @pl.when((c == 1) & has_prior)
        def _():
            fwd[part].wait_recv()

    eye = lax.broadcasted_iota(jnp.int32, (T, T), 0) == lax.broadcasted_iota(jnp.int32, (T, T), 1)

    def build(p):
        for n in range(PIECES[p][0], PIECES[p][0] + PIECES[p][1]):
            i, j = TILES[n]
            rr, cc = slice(T * i, T * i + T), slice(T * j, T * j + T)
            tile = first[rr, cc] + O[rr, cc]
            if i == j:
                mass = mrow[0:1, cc] + mb[0:1, cc]
                tile = tile + jnp.where(eye, jnp.broadcast_to(mass, (T, T)), 0.0)
            D[n] = tile

    def finish_first():
        @pl.when((c == 0) & has_prior)
        def _():
            nxt[2].wait_recv()
            fwd[0].wait_send()
            fwd[1].wait_send()

        @pl.when((c == 1) & has_next)
        def _():
            for copy in nxt:
                copy.wait_send()

        @pl.when((c == 1) & jnp.logical_not(has_next))
        def _():
            first[...] = jnp.zeros((N, N), F32)

    T2[...] = jnp.zeros((2, 2, H, H), F32)

    def step(k, d):
        prev = d // 2
        slot, was = k % 2, (k + 1) % 2
        e = inside(s + sgn * d) & (k < levels)
        e_prev = inside(s + sgn * prev) & (k >= 1)
        e_sib = inside(s - sgn * prev) & (k >= 1)
        kp = jnp.maximum(k - 1, 0)
        peer = s + sgn * d
        peer_prev = s + sgn * prev

        def q_copy(p, level, to):
            o, n = PIECES[p]
            return remote(
                sendQ.at[pl.ds(o, n)],
                recvQ.at[level, pl.ds(o, n)],
                q_send.at[p],
                q_recv.at[level, p],
                to,
                sib,
            )

        def q_forward(p, level):
            o, n = PIECES[p]
            return to_sib(
                recvQ.at[level, pl.ds(o, n)],
                sibQ.at[level, pl.ds(o, n)],
                qf_send.at[p],
                qf_recv.at[level, p],
            )

        def p_copy(h, level, to):
            rows = pl.ds(pl.multiple_of(h * H, H), H)
            return remote(
                sendP.at[rows],
                recvP.at[level + 1, rows],
                p_send.at[h],
                p_recv.at[level, h],
                to,
                sib,
            )

        def v_copy(h, level):
            rows = pl.ds(pl.multiple_of(h * H, H), H)
            return to_sib(VX.at[rows], VY.at[level, rows], v_send.at[h], v_recv.at[level, h])

        def r_copy(level, to):
            return remote(sendR, recvR.at[level], r_send, r_recv.at[level], to, sib)

        def r_forward(level):
            return to_sib(recvR.at[level], sibR.at[level], rf_send, rf_recv.at[level])

        early = (k % 2 == 1) | (k == levels)
        late = jnp.logical_not(early)

        def pass_on(p, now):
            @pl.when(e_prev & now)
            def _():
                q_copy(p, kp, peer_prev).wait_recv()
                q_forward(p, kp).start()

        def take(p):
            o, n = PIECES[p]

            @pl.when(k == 0)
            def _():
                if p in (0, 2):
                    arrive(p // 2)
                build(p)

            pass_on(p, late)

            @pl.when(e_prev)
            def _():
                D[o : o + n] = D[o : o + n] - recvQ[kp, o : o + n]

            @pl.when(e_sib)
            def _():
                q_forward(p, kp).wait_recv()
                D[o : o + n] = D[o : o + n] - sibQ[kp, o : o + n]

            DW[o : o + n] = D[o : o + n]

            @pl.when(e_prev)
            def _():
                q_forward(p, kp).wait_send()

        pass_on(0, early)
        pass_on(1, early)
        take(0)

        def pass_on_rhs(level, stride, on):
            there = s + sgn * stride

            @pl.when(on & inside(there))
            def _():
                r_copy(level, there).wait_recv()
                r_forward(level).start()

        def take_rhs(level, stride, on):
            there = s + sgn * stride

            @pl.when(on & inside(there))
            def _():
                RT[...] = RT[...] + recvR[level]

            @pl.when(on & inside(s - sgn * stride))
            def _():
                r_forward(level).wait_recv()
                RT[...] = RT[...] + sibR[level]

            @pl.when(on & inside(there))
            def _():
                r_forward(level).wait_send()
                r_copy(level, there).wait_send()

        def rhs():
            pass_on_rhs(jnp.maximum(k - 2, 0), d // 4, (k >= 2) & (k % 2 == 1))
            take_rhs(jnp.maximum(k - 2, 0), d // 4, k >= 2)

            @pl.when(k >= 1)
            def _():
                va = dot(RT[:, 0:H], T2[was, 0])
                VR[:, 0:H] = va
                VR[:, H:N] = dot(RT[:, H:N] - dot(va, G[was]), T2[was, 1])
                sendR[...] = dot(VR[...], VX[...])

                @pl.when(e_prev)
                def _():
                    r_copy(kp, peer_prev).start()

        def quarter(i, _):
            h = i // 2
            inv = leaf(DW[7 * h + 2 * (i - 2 * h)], scr)

            @pl.when(i == 0)
            def _():
                take(1)

            @pl.when(i == 2 * h)
            def _():
                T2[slot, h, 0:T, 0:T] = inv
                g = dot(DW[7 * h + 1], inv)
                DW[7 * h + 2] = DW[7 * h + 2] - dot(g, g)
                W[...] = dot(g, inv, NN)

                @pl.when(i == 0)
                def _():
                    pass_on(2, early)

            @pl.when(i == 2 * h + 1)
            def _():
                T2[slot, h, T:H, T:H] = inv
                T2[slot, h, T:H, 0:T] = -dot(inv, W[...], NN)

            @pl.when(i == 1)
            def _():
                pass_on(3, early)
                pass_on_rhs(jnp.maximum(k - 2, 0), d // 4, (k >= 2) & (k % 2 == 0))
                take(2)
                ba = jnp.concatenate(
                    [
                        jnp.concatenate([DW[3], DW[5]], 1),
                        jnp.concatenate([DW[4], DW[6]], 1),
                    ],
                    0,
                )
                g = dot(ba, T2[slot, 0])
                G[slot] = g
                gg = dot(g, g)
                take(3)
                DW[7] = DW[7] - gg[0:T, 0:T]
                DW[8] = DW[8] - gg[T:H, 0:T]
                DW[9] = DW[9] - gg[T:H, T:H]
                rhs()

            return 0

        lax.fori_loop(0, 4, quarter, 0)

        @pl.when(k < levels)
        def _():
            @pl.when(k == 0)
            def _():
                finish_first()

            def solve(h):
                rows = slice(h * H, h * H + H)

                @pl.when(e_prev)
                def _():
                    p_copy(h, kp, peer_prev).wait_recv()

                @pl.when(k >= 1)
                def _():
                    v_copy(h, kp).wait_send()

                va = dot(recvP[k, rows, 0:H], T2[slot, 0])
                VX[rows, 0:H] = va
                VX[rows, H:N] = dot(recvP[k, rows, H:N] - dot(va, G[slot]), T2[slot, 1])

                @pl.when(k < levels - 1)
                def _():
                    v_copy(h, k).start()

            def diagonal(i, j, pieces):
                qq = dot(VX[i * H : i * H + H, :], VX[j * H : j * H + H, :])
                for p in pieces:

                    @pl.when(e_prev)
                    def _():
                        q_copy(p, kp, peer_prev).wait_send()

                    for n in range(PIECES[p][0], PIECES[p][0] + PIECES[p][1]):
                        r0, c0 = TILES[n][0] * T - i * H, TILES[n][1] * T - j * H
                        sendQ[n] = qq[r0 : r0 + T, c0 : c0 + T]

                    @pl.when(e)
                    def _():
                        q_copy(p, k, peer).start()

            solve(0)
            diagonal(0, 0, (0, 1))
            solve(1)
            diagonal(1, 0, (2,))
            diagonal(1, 1, (3,))

        @pl.when(k < levels - 1)
        def _():
            def product(h, _):
                rows = pl.ds(pl.multiple_of(h * H, H), H)
                v_copy(h, k).wait_recv()

                @pl.when(e_prev)
                def _():
                    p_copy(h, kp, peer_prev).wait_send()

                sendP[rows, :] = dot(VY[k, rows, :], VX[...])

                @pl.when(e)
                def _():
                    p_copy(h, k, peer).start()

                @pl.when(jnp.logical_not(e))
                def _():
                    recvP[k + 1, rows, :] = jnp.zeros((H, N), F32)

                return 0

            lax.fori_loop(0, 2, product, 0)

        @pl.when((k == levels - 1) & e_prev)
        def _():
            p_copy(0, kp, peer_prev).wait_send()
            p_copy(1, kp, peer_prev).wait_send()

        @pl.when(k == levels)
        def _():
            pass_on_rhs(kp, prev, k >= 1)
            take_rhs(kp, prev, k >= 1)

        @pl.when((k == levels) & e_prev)
        def _():
            for p in range(len(PIECES)):
                q_copy(p, kp, peer_prev).wait_send()

        return d * 2

    lax.fori_loop(0, levels + 1, step, 1)

    end = levels % 2
    va = dot(RT[own_rt, 0:H], T2[end, 0])
    vb = dot(RT[own_rt, H:N] - dot(va, G[end]), T2[end, 1])
    xb = dot(vb, T2[end, 1], NN)
    xa = dot(va - dot(xb, G[end], NN), T2[end, 0], NN)
    out[0:H, :] = xa.T
    out[H:N, :] = xb.T


def solution(mesh):
    slabs = mesh.shape["slab"]
    levels = (slabs - 1).bit_length()

    def on_device(coupling, tile_pattern, orbital_mass, sources):
        column = lax.axis_index("col")
        pattern = tile_pattern[0]
        mask = jnp.broadcast_to(
            pattern.T[:, None, :, None].astype(F32), (N // T // 2, T, N // T, T)
        ).reshape(H, N)
        rows = lax.broadcasted_iota(jnp.int32, (H, N), 0) + column * H
        cols = lax.broadcasted_iota(jnp.int32, (H, N), 1)
        brow = (rows == cols).astype(F32) + mask * coupling[0].T
        both = jnp.concatenate([orbital_mass[0], orbital_mass[0]])
        mine = (jnp.arange(N) // H == column).astype(F32)
        mrow = jnp.broadcast_to((both * mine)[None], (8, N))
        dma = pltpu.SemaphoreType.DMA
        vmem = pl.BlockSpec(memory_space=pltpu.VMEM)
        x = pl.pallas_call(
            functools.partial(kernel, slabs, levels),
            out_shape=jax.ShapeDtypeStruct((N, T), F32),
            in_specs=[vmem] * 3,
            out_specs=vmem,
            scratch_shapes=[
                pltpu.VMEM((levels, N, N), F32),
                pltpu.VMEM((levels, 10, T, T), F32),
                pltpu.VMEM((levels, 10, T, T), F32),
                pltpu.VMEM((levels, M, N), F32),
                pltpu.VMEM((levels, M, N), F32),
                pltpu.VMEM((levels, N, N), F32),
                pltpu.VMEM((N, N), F32),
                pltpu.VMEM((N, N), F32),
                pltpu.VMEM((M, N), F32),
                pltpu.VMEM((M, N), F32),
                pltpu.VMEM((10, T, T), F32),
                pltpu.VMEM((10, T, T), F32),
                pltpu.VMEM((2, 2, H, H), F32),
                pltpu.VMEM((2, H, H), F32),
                pltpu.VMEM((T, T), F32),
                pltpu.VMEM((18, 8, T), F32),
                pltpu.VMEM((8, N), F32),
                pltpu.VMEM((10, T, T), F32),
                pltpu.VMEM((N, N), F32),
                pltpu.VMEM((M, N), F32),
                dma((3,)),
                dma((3,)),
                dma((3,)),
                dma((3,)),
                dma((2,)),
                dma((2,)),
                dma((2,)),
                dma((levels, 2)),
                dma((len(PIECES),)),
                dma((levels, len(PIECES))),
                dma((len(PIECES),)),
                dma((levels, len(PIECES))),
                dma((2,)),
                dma((levels, 2)),
                dma(()),
                dma((levels,)),
                dma(()),
                dma((levels,)),
            ],
            compiler_params=pltpu.CompilerParams(
                collective_id=0, has_side_effects=True, vmem_limit_bytes=56 << 20
            ),
        )(brow, sources[0], mrow)
        return x[None]

    placed = (
        P("slab", None, "col"),
        P("slab", None, "col"),
        P("slab", "col"),
        P("slab", None, "col"),
    )
    return jax.shard_map(
        on_device, mesh=mesh, in_specs=placed, out_specs=P("slab", None, "col"), check_vma=False
    )
```

```python
import functools

import jax
import jax.numpy as jnp
from jax import lax
from jax.experimental import pallas as pl
from jax.experimental.pallas import tpu as pltpu
from jax.sharding import PartitionSpec as P

F32 = jnp.float32
N = 512
H = 256
T = 128
M = 256
NT = (((1,), (1,)), ((), ()))
NN = (((1,), (0,)), ((), ()))
TILES = ((0, 0), (1, 0), (1, 1), (2, 0), (3, 0), (2, 1), (3, 1), (2, 2), (3, 2), (3, 3))
PIECES = ((0, 1), (1, 2), (3, 4), (7, 3))
MESH = pl.DeviceIdType.MESH


def dot(a, b, dims=NT):
    return lax.dot_general(
        a, b, dims, precision=lax.Precision.HIGHEST, preferred_element_type=F32
    )


def leaf(block, scr):
    rows = [block[8 * i : 8 * i + 8, :] for i in range(16)]
    lane = lax.broadcasted_iota(jnp.int32, (8, T), 1)
    sub = lax.broadcasted_iota(jnp.int32, (8, T), 0)
    out = []
    for J in range(16):
        b = (J % 2) * 9
        own = (lane >= 8 * J) & (lane < 8 * J + 8)
        for j in range(8):
            scr[b + j] = jnp.broadcast_to(rows[J][:, 8 * J + j : 8 * J + j + 1], (8, T))
        scr[b + 8] = jnp.where(own, jnp.where(lane == sub + 8 * J, 1.0, 0.0), rows[J])
        R = [jnp.broadcast_to(scr[b + 8, i : i + 1, :], (8, T)) for i in range(8)]
        E = [[None] * 8 for _ in range(8)]
        for i in range(8):
            for j in range(i + 1):
                E[i][j] = E[j][i] = jnp.broadcast_to(scr[b + j, i : i + 1, :], (8, T))
        V = [None] * 8
        for j in range(0, 8, 2):
            a, c, e = E[j][j], E[j][j + 1], E[j + 1][j + 1]
            q = 1.0 / (a * e - c * c)
            r = c * (1.0 / a)
            V[j] = R[j] * lax.rsqrt(a)
            V[j + 1] = (R[j + 1] - r * R[j]) * lax.rsqrt(e - c * r)
            ia, ic, ie = e * q, c * q, a * q
            R[j], R[j + 1] = ia * R[j] - ic * R[j + 1], ie * R[j + 1] - ic * R[j]
            for k in range(j + 2, 8):
                E[j][k], E[j + 1][k] = (
                    ia * E[j][k] - ic * E[j + 1][k],
                    ie * E[j + 1][k] - ic * E[j][k],
                )
            for i in range(8):
                if i in (j, j + 1):
                    continue
                m0, m1 = E[i][j], E[i][j + 1]
                R[i] = R[i] - (m0 * R[j] + m1 * R[j + 1])
                for k in range(j + 2, 8):
                    if i < j or k >= i:
                        E[i][k] = E[i][k] - (m0 * E[j][k] + m1 * E[j + 1][k])
            for i in range(j + 2, 8):
                for k in range(j + 2, i):
                    E[i][k] = E[k][i]
        for i in range(J + 1, 16):
            t = None
            for k in range(8):
                c = jnp.broadcast_to(rows[i][:, 8 * J + k : 8 * J + k + 1], (8, T)) * R[k]
                t = c if t is None else t + c
            rows[i] = jnp.where(own, 0.0, rows[i]) - t
        z = V[0]
        for r in range(1, 8):
            z = jnp.where(sub == r, V[r], z)
        out.append(jnp.where(lane <= sub + 8 * J, z, 0.0))
    return jnp.concatenate(out, 0)


def kernel(
    slabs,
    levels,
    brow,
    src,
    mrow,
    out,
    recvP,
    recvQ,
    sibQ,
    recvR,
    sibR,
    VY,
    O,
    VX,
    VR,
    RT,
    D,
    DW,
    T2,
    G,
    W,
    scr,
    mb,
    sendQ,
    sendP,
    sendR,
    i_send,
    i_recv,
    n_send,
    n_recv,
    f_send,
    f_recv,
    v_send,
    v_recv,
    q_send,
    q_recv,
    qf_send,
    qf_recv,
    p_send,
    p_recv,
    r_send,
    r_recv,
    rf_send,
    rf_recv,
):
    s = lax.axis_index("slab")
    c = lax.axis_index("col")
    sgn = 2 * c - 1
    sib = 1 - c

    def inside(t):
        return (t >= 0) & (t < slabs)

    def remote(src, dst, ss, rs, slab, col):
        return pltpu.make_async_remote_copy(
            src_ref=src,
            dst_ref=dst,
            send_sem=ss,
            recv_sem=rs,
            device_id={"slab": slab, "col": col},
            device_id_type=MESH,
        )

    barrier = pltpu.get_barrier_semaphore()
    pl.semaphore_signal(barrier, inc=1, device_id={"slab": s, "col": sib}, device_id_type=MESH)
    count = 1
    for k in range(levels):
        peer = s + sgn * 2**k
        here = inside(peer)
        count = count + here.astype(jnp.int32)

        @pl.when(here)
        def _():
            pl.semaphore_signal(
                barrier, inc=1, device_id={"slab": peer, "col": sib}, device_id_type=MESH
            )

    pl.semaphore_wait(barrier, count)

    first = recvP.at[0]
    own_rt = pl.ds(pl.multiple_of(c * T, T), T)
    RT[own_rt, :] = src[...].T
    to_sib = functools.partial(remote, slab=s, col=sib)
    cp_m = to_sib(mrow, mb, i_send.at[0], i_recv.at[0])
    cp_r = to_sib(RT.at[own_rt], RT.at[own_rt], i_send.at[1], i_recv.at[1])
    low, high, full = pl.ds(0, H), pl.ds(H, H), pl.ds(0, N)
    cp_b0 = to_sib(brow, first.at[low], i_send.at[2], i_recv.at[2])
    cp_b1 = to_sib(brow, O.at[high], i_send.at[2], i_recv.at[2])
    parts = ((low, low), (high, full), (low, high))
    nxt = [
        remote(first.at[p], first.at[p], n_send.at[i], n_recv.at[i], s + 1, 0)
        for i, p in enumerate(parts)
    ]
    fwd = [to_sib(first.at[p], O.at[p], f_send.at[i], f_recv.at[i]) for i, p in enumerate(parts[:2])]
    has_next, has_prior = s < slabs - 1, s > 0

    @pl.when(c == 0)
    def _():
        cp_b0.start()
        O[0:H, :] = brow[...]

        @pl.when(s == 0)
        def _():
            first[...] = jnp.zeros((N, N), F32)

    @pl.when(c == 1)
    def _():
        cp_b1.start()
        first[H:N, :] = brow[...]
        cp_b0.wait_recv()

        @pl.when(has_next)
        def _():
            for copy in nxt:
                copy.start()

        @pl.when(s == 0)
        def _():
            O[...] = jnp.zeros((N, N), F32)

    cp_m.start()
    cp_r.start()
    cp_m.wait()
    cp_r.wait()

    @pl.when(c == 0)
    def _():
        cp_b1.wait_recv()
        cp_b0.wait_send()

    @pl.when(c == 1)
    def _():
        cp_b1.wait_send()

    def arrive(part):
        @pl.when((c == 0) & has_prior)
        def _():
            nxt[part].wait_recv()
            fwd[part].start()

        @pl.when((c == 1) & has_prior)
        def _():
            fwd[part].wait_recv()

    eye = lax.broadcasted_iota(jnp.int32, (T, T), 0) == lax.broadcasted_iota(jnp.int32, (T, T), 1)

    def build(p):
        for n in range(PIECES[p][0], PIECES[p][0] + PIECES[p][1]):
            i, j = TILES[n]
            rr, cc = slice(T * i, T * i + T), slice(T * j, T * j + T)
            tile = first[rr, cc] + O[rr, cc]
            if i == j:
                mass = mrow[0:1, cc] + mb[0:1, cc]
                tile = tile + jnp.where(eye, jnp.broadcast_to(mass, (T, T)), 0.0)
            D[n] = tile

    def finish_first():
        @pl.when((c == 0) & has_prior)
        def _():
            nxt[2].wait_recv()
            fwd[0].wait_send()
            fwd[1].wait_send()

        @pl.when((c == 1) & has_next)
        def _():
            for copy in nxt:
                copy.wait_send()

        @pl.when((c == 1) & jnp.logical_not(has_next))
        def _():
            first[...] = jnp.zeros((N, N), F32)

    T2[...] = jnp.zeros((2, 2, H, H), F32)

    def step(k, d):
        prev = d // 2
        slot, was = k % 2, (k + 1) % 2
        e = inside(s + sgn * d) & (k < levels)
        e_prev = inside(s + sgn * prev) & (k >= 1)
        e_sib = inside(s - sgn * prev) & (k >= 1)
        kp = jnp.maximum(k - 1, 0)
        peer = s + sgn * d
        peer_prev = s + sgn * prev

        def q_copy(p, level, to):
            o, n = PIECES[p]
            return remote(
                sendQ.at[pl.ds(o, n)],
                recvQ.at[level, pl.ds(o, n)],
                q_send.at[p],
                q_recv.at[level, p],
                to,
                sib,
            )

        def q_forward(p, level):
            o, n = PIECES[p]
            return to_sib(
                recvQ.at[level, pl.ds(o, n)],
                sibQ.at[level, pl.ds(o, n)],
                qf_send.at[p],
                qf_recv.at[level, p],
            )

        def p_copy(h, level, to):
            rows = pl.ds(pl.multiple_of(h * H, H), H)
            return remote(
                sendP.at[rows],
                recvP.at[level + 1, rows],
                p_send.at[h],
                p_recv.at[level, h],
                to,
                sib,
            )

        def v_copy(h, level):
            rows = pl.ds(pl.multiple_of(h * H, H), H)
            return to_sib(VX.at[rows], VY.at[level, rows], v_send.at[h], v_recv.at[level, h])

        def r_copy(level, to):
            return remote(sendR, recvR.at[level], r_send, r_recv.at[level], to, sib)

        def r_forward(level):
            return to_sib(recvR.at[level], sibR.at[level], rf_send, rf_recv.at[level])

        def take(p):
            o, n = PIECES[p]

            @pl.when(k == 0)
            def _():
                if p in (0, 2):
                    arrive(p // 2)
                build(p)

            @pl.when(e_prev)
            def _():
                q_copy(p, kp, peer_prev).wait_recv()
                q_forward(p, kp).start()
                D[o : o + n] = D[o : o + n] - recvQ[kp, o : o + n]

            @pl.when(e_sib)
            def _():
                q_forward(p, kp).wait_recv()
                D[o : o + n] = D[o : o + n] - sibQ[kp, o : o + n]

            DW[o : o + n] = D[o : o + n]

            @pl.when(e_prev)
            def _():
                q_forward(p, kp).wait_send()

        take(0)

        def take_rhs(level, stride, on):
            there = s + sgn * stride

            @pl.when(on & inside(there))
            def _():
                r_copy(level, there).wait_recv()
                r_forward(level).start()
                RT[...] = RT[...] + recvR[level]

            @pl.when(on & inside(s - sgn * stride))
            def _():
                r_forward(level).wait_recv()
                RT[...] = RT[...] + sibR[level]

            @pl.when(on & inside(there))
            def _():
                r_forward(level).wait_send()
                r_copy(level, there).wait_send()

        def rhs():
            take_rhs(jnp.maximum(k - 2, 0), d // 4, k >= 2)

            @pl.when(k >= 1)
            def _():
                va = dot(RT[:, 0:H], T2[was, 0])
                VR[:, 0:H] = va
                VR[:, H:N] = dot(RT[:, H:N] - dot(va, G[was]), T2[was, 1])
                sendR[...] = dot(VR[...], VX[...])

                @pl.when(e_prev)
                def _():
                    r_copy(kp, peer_prev).start()

        def quarter(i, _):
            h = i // 2
            inv = leaf(DW[7 * h + 2 * (i - 2 * h)], scr)

            @pl.when(i == 0)
            def _():
                take(1)

            @pl.when(i == 2 * h)
            def _():
                T2[slot, h, 0:T, 0:T] = inv
                g = dot(DW[7 * h + 1], inv)
                DW[7 * h + 2] = DW[7 * h + 2] - dot(g, g)
                W[...] = dot(g, inv, NN)

            @pl.when(i == 2 * h + 1)
            def _():
                T2[slot, h, T:H, T:H] = inv
                T2[slot, h, T:H, 0:T] = -dot(inv, W[...], NN)

            @pl.when(i == 1)
            def _():
                rhs()
                take(2)
                ba = jnp.concatenate(
                    [
                        jnp.concatenate([DW[3], DW[5]], 1),
                        jnp.concatenate([DW[4], DW[6]], 1),
                    ],
                    0,
                )
                g = dot(ba, T2[slot, 0])
                G[slot] = g
                gg = dot(g, g)
                take(3)
                DW[7] = DW[7] - gg[0:T, 0:T]
                DW[8] = DW[8] - gg[T:H, 0:T]
                DW[9] = DW[9] - gg[T:H, T:H]

            return 0

        lax.fori_loop(0, 4, quarter, 0)

        @pl.when(k < levels)
        def _():
            @pl.when(k == 0)
            def _():
                finish_first()

            def solve(h):
                rows = slice(h * H, h * H + H)

                @pl.when(e_prev)
                def _():
                    p_copy(h, kp, peer_prev).wait_recv()

                @pl.when(k >= 1)
                def _():
                    v_copy(h, kp).wait_send()

                va = dot(recvP[k, rows, 0:H], T2[slot, 0])
                VX[rows, 0:H] = va
                VX[rows, H:N] = dot(recvP[k, rows, H:N] - dot(va, G[slot]), T2[slot, 1])

                @pl.when(k < levels - 1)
                def _():
                    v_copy(h, k).start()

            def diagonal(i, j, pieces):
                qq = dot(VX[i * H : i * H + H, :], VX[j * H : j * H + H, :])
                for p in pieces:

                    @pl.when(e_prev)
                    def _():
                        q_copy(p, kp, peer_prev).wait_send()

                    for n in range(PIECES[p][0], PIECES[p][0] + PIECES[p][1]):
                        r0, c0 = TILES[n][0] * T - i * H, TILES[n][1] * T - j * H
                        sendQ[n] = qq[r0 : r0 + T, c0 : c0 + T]

                    @pl.when(e)
                    def _():
                        q_copy(p, k, peer).start()

            solve(0)
            diagonal(0, 0, (0, 1))
            solve(1)
            diagonal(1, 0, (2,))
            diagonal(1, 1, (3,))

        @pl.when(k < levels - 1)
        def _():
            def product(h, _):
                rows = pl.ds(pl.multiple_of(h * H, H), H)
                v_copy(h, k).wait_recv()

                @pl.when(e_prev)
                def _():
                    p_copy(h, kp, peer_prev).wait_send()

                sendP[rows, :] = dot(VY[k, rows, :], VX[...])

                @pl.when(e)
                def _():
                    p_copy(h, k, peer).start()

                @pl.when(jnp.logical_not(e))
                def _():
                    recvP[k + 1, rows, :] = jnp.zeros((H, N), F32)

                return 0

            lax.fori_loop(0, 2, product, 0)

        @pl.when((k == levels - 1) & e_prev)
        def _():
            p_copy(0, kp, peer_prev).wait_send()
            p_copy(1, kp, peer_prev).wait_send()

        @pl.when(k == levels)
        def _():
            take_rhs(kp, prev, k >= 1)

        @pl.when((k == levels) & e_prev)
        def _():
            for p in range(len(PIECES)):
                q_copy(p, kp, peer_prev).wait_send()

        return d * 2

    lax.fori_loop(0, levels + 1, step, 1)

    end = levels % 2
    va = dot(RT[own_rt, 0:H], T2[end, 0])
    vb = dot(RT[own_rt, H:N] - dot(va, G[end]), T2[end, 1])
    xb = dot(vb, T2[end, 1], NN)
    xa = dot(va - dot(xb, G[end], NN), T2[end, 0], NN)
    out[0:H, :] = xa.T
    out[H:N, :] = xb.T


def solution(mesh):
    slabs = mesh.shape["slab"]
    levels = (slabs - 1).bit_length()

    def on_device(coupling, tile_pattern, orbital_mass, sources):
        column = lax.axis_index("col")
        pattern = tile_pattern[0]
        mask = jnp.broadcast_to(
            pattern.T[:, None, :, None].astype(F32), (N // T // 2, T, N // T, T)
        ).reshape(H, N)
        rows = lax.broadcasted_iota(jnp.int32, (H, N), 0) + column * H
        cols = lax.broadcasted_iota(jnp.int32, (H, N), 1)
        brow = (rows == cols).astype(F32) + mask * coupling[0].T
        both = jnp.concatenate([orbital_mass[0], orbital_mass[0]])
        mine = (jnp.arange(N) // H == column).astype(F32)
        mrow = jnp.broadcast_to((both * mine)[None], (8, N))
        dma = pltpu.SemaphoreType.DMA
        vmem = pl.BlockSpec(memory_space=pltpu.VMEM)
        x = pl.pallas_call(
            functools.partial(kernel, slabs, levels),
            out_shape=jax.ShapeDtypeStruct((N, T), F32),
            in_specs=[vmem] * 3,
            out_specs=vmem,
            scratch_shapes=[
                pltpu.VMEM((levels, N, N), F32),
                pltpu.VMEM((levels, 10, T, T), F32),
                pltpu.VMEM((levels, 10, T, T), F32),
                pltpu.VMEM((levels, M, N), F32),
                pltpu.VMEM((levels, M, N), F32),
                pltpu.VMEM((levels, N, N), F32),
                pltpu.VMEM((N, N), F32),
                pltpu.VMEM((N, N), F32),
                pltpu.VMEM((M, N), F32),
                pltpu.VMEM((M, N), F32),
                pltpu.VMEM((10, T, T), F32),
                pltpu.VMEM((10, T, T), F32),
                pltpu.VMEM((2, 2, H, H), F32),
                pltpu.VMEM((2, H, H), F32),
                pltpu.VMEM((T, T), F32),
                pltpu.VMEM((18, 8, T), F32),
                pltpu.VMEM((8, N), F32),
                pltpu.VMEM((10, T, T), F32),
                pltpu.VMEM((N, N), F32),
                pltpu.VMEM((M, N), F32),
                dma((3,)),
                dma((3,)),
                dma((3,)),
                dma((3,)),
                dma((2,)),
                dma((2,)),
                dma((2,)),
                dma((levels, 2)),
                dma((len(PIECES),)),
                dma((levels, len(PIECES))),
                dma((len(PIECES),)),
                dma((levels, len(PIECES))),
                dma((2,)),
                dma((levels, 2)),
                dma(()),
                dma((levels,)),
                dma(()),
                dma((levels,)),
            ],
            compiler_params=pltpu.CompilerParams(
                collective_id=0, has_side_effects=True, vmem_limit_bytes=56 << 20
            ),
        )(brow, sources[0], mrow)
        return x[None]

    placed = (
        P("slab", None, "col"),
        P("slab", None, "col"),
        P("slab", "col"),
        P("slab", None, "col"),
    )
    return jax.shard_map(
        on_device, mesh=mesh, in_specs=placed, out_specs=P("slab", None, "col"), check_vma=False
    )
```
